512 devices in a mesh: seq: 32 (over z, core), head: 16 (over x, y).
Axes of the slice: x: 4, y: 4, z: 16, core: 2. Of those that a mesh axis runs over, the one named last changes fastest.
Arguments:
- tokens: bfloat16 [8192, 4096], P('seq', 'head'), may hold values from -40 to 40
- norm_gain: float32 [4096], replicated, may hold values from 1.5 to 8
- w_qkv: bfloat16 [4096, 3, 2048], P(None, None, 'head'), may hold values from -0.09375 to 0.09375
- w_out: bfloat16 [2048, 4096], P('head'), may hold values from -0.75 to 0.75
- span_order: int32 [64], replicated, may hold values from 0 to 63, each once
- frame_id: int32 [8192], replicated, may hold values from 0 to 63, never falling along the last dimension, each value on 1 to 256 neighbouring positions
- camera_id: int32 [8192], replicated, may hold values from 0 to 5
Outputs:
- mixed: bfloat16 [8192, 4096], P('seq', 'head')
The draws below stay inside these ranges and needn't reach their ends.
Inputs may be any that keep to these rules, and one draw needn't show every extreme that they name: `span_order`: each of the 64 spans appears once. `frame_id`: never falls along the sequence; every frame has 1 to 256 positions and one has exactly 256.
All inputs are finite; a program needn't handle non-finite values.
Results may differ from the reference program's by a relative error of at most 0.015.
The reference program's roundings to bfloat16 on the way count: a program that leaves them out, or rounds other values in their place, can miss the bound.
Values may be sent and summed in bfloat16 or wider, within the bound.
No kernel may reach another device: no remote copies, remote signals or barrier semaphores. Data moves between devices by JAX's collectives and lax.ppermute only.
A program may use at most 64 MiB of HBM per device.

```python
import math
import jax
import jax.numpy as jnp
import numpy as np
from jax import lax

D = 4096
HD = 128
HEADS = 16
TOK_DEV = 256
SEQ_LEN = 8192
SPANS = 64
FRAMES = 64
FRAME_MOST = 256
CAMERAS = 6
N_SEQ = 32


def draw_tokens(key, part):
    key_rows, key_cols, key_base = jax.random.split(jax.random.fold_in(key, 11), 3)
    row_scale = jnp.exp(jax.random.uniform(key_rows, (SEQ_LEN, 1), jnp.float32, math.log(0.3), math.log(3.0)))
    col_scale = jnp.exp(jax.random.uniform(key_cols, (1, D), jnp.float32, math.log(0.5), math.log(2.0)))
    base_values = jax.random.normal(key_base, (SEQ_LEN, D), jnp.float32)
    values = jnp.clip(base_values * row_scale * col_scale, -40.0, 40.0)
    return values.astype(jnp.bfloat16)


def draw_norm_gain(key, part):
    key_gain = jax.random.fold_in(key, 23)
    lower, upper = (math.log(1.5), math.log(3.0))
    return jnp.exp(jax.random.uniform(key_gain, (D,), jnp.float32, lower, upper))


def place_ends(result, stream_key, smallest, largest):
    place = [jax.random.randint(jax.random.fold_in(stream_key, axis), (), 0, length) for axis, length in enumerate(result.shape)]
    longest = result.shape.index(max(result.shape))
    neighbour = place[:longest] + [(place[longest] + 1) % result.shape[longest]] + place[longest + 1:]
    return result.at[tuple(place)].set(smallest).at[tuple(neighbour)].set(largest)


def strengthened(drawn, key, source, target, blocks, factor):
    owner, partner = [(jnp.arange(drawn.shape[axis_at]) // (drawn.shape[axis_at] // blocks)).reshape([-1 if axis == axis_at else 1 for axis in range(drawn.ndim)]) for axis_at in (source, target)]
    chosen = jax.random.permutation(key, blocks)[partner]
    strong = (owner == chosen) | (owner == (partner + blocks // 2) % blocks)
    return jnp.where(strong, factor * drawn, drawn)


def block_scale(stream_key, shape, pieces, least, high):
    factor_of, own = 1.0, jax.random.fold_in(stream_key, 6)
    for position, blocks in pieces:
        heights = jnp.exp(jax.random.uniform(jax.random.fold_in(own, position), (blocks,), jnp.float32, least / len(pieces), high / len(pieces)))
        factor_of = factor_of * jnp.repeat(heights, shape[position] // blocks).reshape([-1 if axis == position else 1 for axis in range(len(shape))])
    return factor_of


def profile(amount, total, reach, skew):
    weights = [(1 << 20) // math.isqrt(grade ** skew) + 1 for grade in range(2, amount + 1)]
    surplus, given = total - reach - (amount - 1), [1] * (amount - 1)
    while surplus > 0:
        candidates = [i for i in range(amount - 1) if given[i] < reach]
        whole, remaining = sum([weights[i] for i in candidates]), surplus
        for i in candidates:
            addition = min(reach - given[i], max(1, remaining * weights[i] // whole), surplus)
            given[i] = given[i] + addition
            surplus = surplus - addition
    return np.array([reach] + given)


def ragged(own_key, count, total, most, skew):
    if count == 2:
        one = jax.random.randint(own_key, (), max(1, total - most), min(most, total - 1) + 1)
        return jnp.stack([one, total - one])
    tallies = jnp.asarray(profile(count, total, most, skew), jnp.int32)
    twos = (count - 1) // 2
    donor, sink = tallies[1:1 + 2 * twos:2], tallies[2:2 + 2 * twos:2]
    room = jnp.minimum(donor - 1, most - sink)
    passed = jax.random.randint(jax.random.fold_in(own_key, 1), (twos,), 0, 1 << 20) % (room + 1)
    tallies = tallies.at[1:1 + 2 * twos:2].set(donor - passed).at[2:2 + 2 * twos:2].set(sink + passed)
    return tallies[jax.random.permutation(jax.random.fold_in(own_key, 2), count)]


def centred(rng, dims, deviation, bound, pieces=(), kind=jnp.bfloat16):
    gain = block_scale(rng, dims, pieces, -0.22, 0.18) if pieces else 1.0
    array = jax.random.normal(rng, dims, jnp.float32) * deviation * gain
    return jnp.minimum(jnp.maximum(array, -bound), bound).astype(kind)


def bell_draw_with(own_key, shape, scale, most, pieces, heavy, kind=jnp.bfloat16):
    entries = scale * jax.random.normal(own_key, shape, jnp.float32)
    if pieces:
        entries = entries * block_scale(own_key, shape, pieces, -0.22, 0.18)
    return jnp.clip(strengthened(entries, jax.random.fold_in(own_key, 3), *heavy), -most, most).astype(kind)


def setup_inputs(seed: int = 0) -> dict:
    seeds = jax.random.split(jax.random.key(seed), 8)
    return {
        "tokens": draw_tokens(jax.random.fold_in(seeds[7], 71), 0),
        "norm_gain": draw_norm_gain(jax.random.fold_in(seeds[7], 71), 0),
        "w_qkv": centred(seeds[2], (D, 3, HEADS * HD), D ** -0.5, 0.09375, ((2, 16),)),
        "w_out": bell_draw_with(seeds[3], (HEADS * HD, D), HD ** -0.5, 0.75, ((0, 16),), (0, 1, 16, 2.0)),
        "span_order": jax.random.permutation(seeds[4], SPANS).astype(jnp.int32),
        "frame_id": jnp.searchsorted(jnp.cumsum(ragged(seeds[5], FRAMES, SEQ_LEN, FRAME_MOST, 1)), jnp.arange(SEQ_LEN), side="right").astype(jnp.int32),
        "camera_id": place_ends(jax.random.randint(seeds[6], (SEQ_LEN,), 0, CAMERAS), jax.random.fold_in(seeds[6], 1), 0, CAMERAS - 1).astype(jnp.int32),
    }


epsilon = 1e-06

def stored_order(id_table, span_order):
    span_count = span_order.shape[0]
    return id_table.reshape(span_count, -1)[span_order].reshape(-1)

def visible_pairs(query_frames, query_cameras, key_frames, key_cameras):
    earlier = key_frames[None, :] < query_frames[:, None]
    same_view = (key_frames[None, :] == query_frames[:, None]) & (key_cameras[None, :] == query_cameras[:, None])
    return earlier | same_view

def reference(tokens, norm_gain, w_qkv, w_out, span_order, frame_id, camera_id):
    frames = stored_order(frame_id, span_order)
    cameras = stored_order(camera_id, span_order)
    widened = tokens.astype(jnp.float32)
    inverse = lax.rsqrt(lax.optimization_barrier(jnp.mean(widened * widened, axis=1, keepdims=True)) + epsilon)
    normed = (widened * inverse * norm_gain).astype(jnp.bfloat16)
    score_scale = HD ** (-0.5)

    def head_output(head_index, running):
        column_start = head_index.astype(jnp.int32) * HD
        columns = lax.dynamic_slice_in_dim(w_qkv, column_start, HD, 2).reshape(D, 3 * HD)
        projected = jnp.dot(normed, columns, preferred_element_type=jnp.float32).astype(jnp.bfloat16)
        queries = projected[:, :HD]
        key_rows = projected[:, HD:2 * HD]
        value_rows = projected[:, 2 * HD:]

        def query_block(block_index):
            first_row = block_index.astype(jnp.int32) * TOK_DEV
            block_queries = lax.dynamic_slice_in_dim(queries, first_row, TOK_DEV, 0)
            block_frames = lax.dynamic_slice_in_dim(frames, first_row, TOK_DEV, 0)
            block_cameras = lax.dynamic_slice_in_dim(cameras, first_row, TOK_DEV, 0)
            scores = jnp.dot(block_queries, key_rows.T, preferred_element_type=jnp.float32) * score_scale
            allowed = visible_pairs(block_frames, block_cameras, frames, cameras)
            row_best = lax.optimization_barrier(jnp.max(jnp.where(allowed, scores, -jnp.inf), axis=1, keepdims=True))
            weights = jnp.exp(jnp.where(allowed, scores - row_best, -jnp.inf))
            weight_sum = lax.optimization_barrier(jnp.sum(weights, axis=1, keepdims=True))
            weighted = jnp.dot(weights.astype(jnp.bfloat16), value_rows, preferred_element_type=jnp.float32)
            return (weighted / weight_sum).astype(jnp.bfloat16)
        attended = lax.map(query_block, jnp.arange(N_SEQ, dtype=jnp.int32)).reshape(SEQ_LEN, HD)
        out_rows = lax.dynamic_slice_in_dim(w_out, column_start, HD, 0)
        head_part = jnp.dot(attended, out_rows, preferred_element_type=jnp.float32).astype(jnp.bfloat16)
        head_part = lax.optimization_barrier(head_part)
        return running + head_part.astype(jnp.float32)
    summed = lax.fori_loop(0, HEADS, head_output, jnp.zeros((SEQ_LEN, D), jnp.float32))
    return summed.astype(jnp.bfloat16)
```

```python
import jax
import jax.numpy as jnp
from jax import lax
from jax.experimental import pallas as pl
from jax.experimental.pallas import tpu as pltpu
from jax.sharding import PartitionSpec as P

D = 4096
HD = 128
ROWS = 256
SPAN = 128
BLOCK_Z = 4
MASKED = -1e30
EPSILON = 1e-06
LOG2_E = 1.4426950408889634
SCALE = HD**-0.5 * LOG2_E
PART_ROWS = HD + 16


def project_kernel(x_ref, gain_ref, w_ref, q_ref, kv_ref, inv_ref, acc_ref):
    step = pl.program_id(0)
    blocks = x_ref.shape[0]
    per_step = blocks // pl.num_programs(0)

    @pl.when(step == 0)
    def _():
        total = jnp.zeros((ROWS, x_ref.shape[2]), jnp.float32)
        for j in range(blocks):
            piece = x_ref[j].astype(jnp.float32)
            total = total + piece * piece
        mean = jnp.sum(total, axis=1, keepdims=True) * (1.0 / D)
        inv_ref[...] = jnp.broadcast_to(lax.rsqrt(mean + EPSILON), inv_ref.shape)
        acc_ref[...] = jnp.zeros_like(acc_ref)

    width = x_ref.shape[2]
    inverse = jnp.concatenate([inv_ref[...]] * (width // 128), axis=1)
    sums = acc_ref[...]
    for i in range(per_step):
        piece = x_ref[step * per_step + i].astype(jnp.float32)
        gain = gain_ref[:, i * width : (i + 1) * width]
        normed = (piece * inverse * gain).astype(jnp.bfloat16)
        rows = slice(i * width, (i + 1) * width)
        weights = jnp.concatenate([w_ref[0, rows], w_ref[1, rows], w_ref[2, rows]], axis=1)
        sums = sums + jnp.dot(normed, weights, preferred_element_type=jnp.float32)
    acc_ref[...] = sums

    @pl.when(step == pl.num_programs(0) - 1)
    def _():
        done = sums.astype(jnp.bfloat16)
        q_ref[...] = done[:, :HD]
        kv_ref[...] = done[:, HD:]


def project(x, gain, w):
    blocks, _, width = x.shape
    steps = 4
    depth = D // steps
    return pl.pallas_call(
        project_kernel,
        grid=(steps,),
        in_specs=[
            pl.BlockSpec((blocks, ROWS, width), lambda s: (0, 0, 0)),
            pl.BlockSpec((1, depth), lambda s: (0, s)),
            pl.BlockSpec((3, depth, HD), lambda s: (0, s, 0)),
        ],
        out_specs=[
            pl.BlockSpec((ROWS, HD), lambda s: (0, 0)),
            pl.BlockSpec((ROWS, 2 * HD), lambda s: (0, 0)),
        ],
        out_shape=[
            jax.ShapeDtypeStruct((ROWS, HD), jnp.bfloat16),
            jax.ShapeDtypeStruct((ROWS, 2 * HD), jnp.bfloat16),
        ],
        scratch_shapes=[
            pltpu.VMEM((ROWS, 128), jnp.float32),
            pltpu.VMEM((ROWS, 3 * HD), jnp.float32),
        ],
        name="project",
    )(x, gain, w)


def attend_kernel(q_ref, qcode_ref, kv_ref, kcode_ref, out_ref, vt_ref):
    keys = kv_ref.shape[0] * ROWS

    @pl.when(pl.program_id(0) == 0)
    def _():
        for j in range(kv_ref.shape[0]):
            vt_ref[:, j * ROWS : (j + 1) * ROWS] = jnp.transpose(kv_ref[j][:, HD:])

    key_rows = kv_ref[...].reshape(keys, 2 * HD)[:, :HD]
    raw = lax.dot_general(
        key_rows, q_ref[0], (((1,), (1,)), ((), ())), preferred_element_type=jnp.float32
    )
    qcode = qcode_ref[0]
    kcode = jnp.concatenate([kcode_ref[...]] * (ROWS // 128), axis=1)
    seen = (kcode < (qcode & -8)) | (kcode == qcode)
    scores = jnp.where(seen, raw * SCALE, MASKED)
    best = jnp.max(scores, axis=0, keepdims=True)
    weights = jnp.exp2(scores - best)
    total = jnp.sum(weights, axis=0, keepdims=True)
    mixed = jnp.dot(vt_ref[...], weights.astype(jnp.bfloat16), preferred_element_type=jnp.float32)
    out_ref[0, :HD] = (mixed / total).astype(jnp.bfloat16)
    level = best + jnp.log2(total)
    high = level.astype(jnp.bfloat16).astype(jnp.float32)
    rest = level - high
    middle = rest.astype(jnp.bfloat16).astype(jnp.float32)
    low = rest - middle
    row = lax.broadcasted_iota(jnp.int32, (16, ROWS), 0)
    stats = jnp.where(row == 0, high, jnp.where(row == 1, middle, jnp.where(row == 2, low, 0.0)))
    out_ref[0, HD:] = stats.astype(jnp.bfloat16)


def attend(q, qcode, kv, kcode):
    groups = q.shape[0]
    keys = kv.shape[0] * ROWS
    return pl.pallas_call(
        attend_kernel,
        grid=(groups,),
        in_specs=[
            pl.BlockSpec((1, ROWS, HD), lambda i: (i, 0, 0)),
            pl.BlockSpec((1, 1, ROWS), lambda i: (i, 0, 0)),
            pl.BlockSpec(kv.shape, lambda i: (0, 0, 0)),
            pl.BlockSpec((keys, 128), lambda i: (0, 0)),
        ],
        out_specs=pl.BlockSpec((1, PART_ROWS, ROWS), lambda i: (i, 0, 0)),
        out_shape=jax.ShapeDtypeStruct((groups, PART_ROWS, ROWS), jnp.bfloat16),
        scratch_shapes=[pltpu.VMEM((HD, keys), jnp.bfloat16)],
        name="attend",
    )(q, qcode, kv, kcode)


def combine_kernel(part_ref, out_ref):
    groups = part_ref.shape[0]
    levels = []
    for j in range(groups):
        stats = part_ref[j, HD:].astype(jnp.float32)
        levels.append(stats[0:1] + stats[1:2] + stats[2:3])
    best = levels[0]
    for level in levels[1:]:
        best = jnp.maximum(best, level)
    total = jnp.zeros_like(best)
    mixed = jnp.zeros((HD, ROWS), jnp.float32)
    for j in range(groups):
        share = jnp.exp2(levels[j] - best)
        total = total + share
        mixed = mixed + share * part_ref[j, :HD].astype(jnp.float32)
    out_ref[...] = jnp.transpose(mixed / total).astype(jnp.bfloat16)


def combine(parts):
    return pl.pallas_call(
        combine_kernel,
        out_shape=jax.ShapeDtypeStruct((ROWS, HD), jnp.bfloat16),
        name="combine",
    )(parts)


def output_kernel(attended_ref, w_ref, out_ref):
    total = jnp.zeros(out_ref.shape, jnp.float32)
    for h in range(attended_ref.shape[0]):
        head_out = jnp.dot(attended_ref[h], w_ref[h], preferred_element_type=jnp.float32)
        total = total + head_out.astype(jnp.bfloat16).astype(jnp.float32)
    out_ref[...] = total.astype(jnp.bfloat16)


def output(attended, w):
    return pl.pallas_call(
        output_kernel,
        out_shape=jax.ShapeDtypeStruct((ROWS, w.shape[2]), jnp.bfloat16),
        name="output",
    )(attended, w)


def send_to_all(array, axis, count, groups=None):
    copies = jnp.broadcast_to(array[None], (count,) + array.shape)
    return lax.all_to_all(copies, axis, 0, 0, axis_index_groups=groups)


def make_on_device(n_seq, n_head):
    group = 2 * BLOCK_Z
    near = [[g * group + i for i in range(group)] for g in range(n_seq // group)]
    far = [[g * group + i for g in range(n_seq // group)] for i in range(group)]
    far_count = n_seq // group

    def on_device(tokens, norm_gain, w_qkv, w_out, span_order, frame_id, camera_id):
        columns = tokens.shape[1]
        gathered = send_to_all(tokens, "head", n_head)
        w_split = w_out.reshape(HD, n_head, columns).transpose(1, 0, 2)
        gathered, w_split = lax.optimization_barrier((gathered, w_split))
        w_columns = lax.all_to_all(w_split, "head", 0, 0)

        queries, kv = project(gathered, norm_gain.reshape(1, D), w_qkv.transpose(1, 0, 2))

        code = (frame_id * 8 + camera_id).reshape(-1, SPAN)[span_order]
        code = code.reshape(n_seq // group, group, ROWS)
        place = lax.axis_index("seq")
        query_code = lax.dynamic_index_in_dim(code, place // group, 0, keepdims=False)
        key_code = lax.dynamic_index_in_dim(code, place % group, 1, keepdims=False)
        key_code = jnp.broadcast_to(key_code.reshape(-1, 1), (far_count * ROWS, 128))

        all_queries = lax.all_gather(queries, "seq", axis_index_groups=near)
        all_kv = send_to_all(kv, "seq", far_count, far)
        parts = attend(all_queries, query_code[:, None, :], all_kv, key_code)
        parts = lax.all_to_all(parts, "seq", 0, 0, axis_index_groups=near)
        attended = combine(parts)
        all_attended = send_to_all(attended, "head", n_head)
        return output(all_attended, w_columns)

    return on_device


def solution(mesh):
    placed = (P("seq", "head"), P(), P(None, None, "head"), P("head", None), P(), P(), P())
    return jax.shard_map(
        make_on_device(mesh.shape["seq"], mesh.shape["head"]),
        mesh=mesh,
        in_specs=placed,
        out_specs=P("seq", "head"),
        check_vma=False,
    )
```

```python
import jax
import jax.numpy as jnp
from jax import lax
from jax.experimental import pallas as pl
from jax.experimental.pallas import tpu as pltpu
from jax.sharding import PartitionSpec as P


D = 4096
HD = 128
ROWS = 256
SPAN = 128
CORES = 2
BLOCK_Z = 4
GRANT = 16 << 20
MASKED = -1e30
EPSILON = 1e-06
LOG2_E = 1.4426950408889634
SCALE = HD**-0.5 * LOG2_E
PART_ROWS = HD + 16


def project_kernel(x_ref, gain_ref, w_ref, q_ref, kv_ref, inv_ref, acc_ref):
    step = pl.program_id(0)
    blocks = x_ref.shape[0]
    per_step = blocks // pl.num_programs(0)

    @pl.when(step == 0)
    def _():
        total = jnp.zeros((ROWS, x_ref.shape[2]), jnp.float32)
        for j in range(blocks):
            piece = x_ref[j].astype(jnp.float32)
            total = total + piece * piece
        mean = jnp.sum(total, axis=1, keepdims=True) * (1.0 / D)
        inv_ref[...] = jnp.broadcast_to(lax.rsqrt(mean + EPSILON), inv_ref.shape)
        acc_ref[...] = jnp.zeros_like(acc_ref)

    width = x_ref.shape[2]
    inverse = jnp.concatenate([inv_ref[...]] * (width // 128), axis=1)
    sums = acc_ref[...]
    for i in range(per_step):
        piece = x_ref[step * per_step + i].astype(jnp.float32)
        gain = gain_ref[:, i * width : (i + 1) * width]
        normed = (piece * inverse * gain).astype(jnp.bfloat16)
        rows = slice(i * width, (i + 1) * width)
        weights = jnp.concatenate([w_ref[0, rows], w_ref[1, rows], w_ref[2, rows]], axis=1)
        sums = sums + jnp.dot(normed, weights, preferred_element_type=jnp.float32)
    acc_ref[...] = sums

    @pl.when(step == pl.num_programs(0) - 1)
    def _():
        done = sums.astype(jnp.bfloat16)
        q_ref[...] = done[:, :HD]
        kv_ref[...] = done[:, HD:]


def project(x, gain, w):
    blocks, _, width = x.shape
    steps = 4
    depth = D // steps
    return pl.pallas_call(
        project_kernel,
        grid=(steps,),
        in_specs=[
            pl.BlockSpec((blocks, ROWS, width), lambda s: (0, 0, 0)),
            pl.BlockSpec((1, depth), lambda s: (0, s)),
            pl.BlockSpec((3, depth, HD), lambda s: (0, s, 0)),
        ],
        out_specs=[
            pl.BlockSpec((ROWS, HD), lambda s: (0, 0)),
            pl.BlockSpec((ROWS, 2 * HD), lambda s: (0, 0)),
        ],
        out_shape=[
            jax.ShapeDtypeStruct((ROWS, HD), jnp.bfloat16),
            jax.ShapeDtypeStruct((ROWS, 2 * HD), jnp.bfloat16),
        ],
        scratch_shapes=[
            pltpu.VMEM((ROWS, 128), jnp.float32),
            pltpu.VMEM((ROWS, 3 * HD), jnp.float32),
        ],
        compiler_params=pltpu.CompilerParams(vmem_limit_bytes=GRANT),
        name="project",
    )(x, gain, w)


def attend_kernel(q_ref, qcode_ref, own_ref, other_ref, kcode_ref, out_ref, vt_ref):
    count = own_ref.shape[0]

    @pl.when(pl.program_id(0) == 0)
    def _():
        for part, ref in enumerate((own_ref, other_ref)):
            for j in range(count):
                at = (part * count + j) * ROWS
                vt_ref[:, at : at + ROWS] = jnp.transpose(ref[j][:, HD:])

    qcode = qcode_ref[0]
    qbase = qcode & -8
    queries = q_ref[0]
    scores = []
    for part, ref in enumerate((own_ref, other_ref)):
        for j in range(count):
            at = (part * count + j) * ROWS
            raw = lax.dot_general(
                ref[j][:, :HD],
                queries,
                (((1,), (1,)), ((), ())),
                preferred_element_type=jnp.float32,
            )
            code = kcode_ref[at : at + ROWS, :]
            kcode = jnp.concatenate([code] * (ROWS // 128), axis=1)
            seen = (kcode < qbase) | (kcode == qcode)
            scores.append(jnp.where(seen, raw * SCALE, MASKED))
    scores = jnp.concatenate(scores, axis=0)
    best = jnp.max(scores, axis=0, keepdims=True)
    weights = jnp.exp2(scores - best)
    total = jnp.sum(weights, axis=0, keepdims=True)
    mixed = jnp.dot(vt_ref[...], weights.astype(jnp.bfloat16), preferred_element_type=jnp.float32)
    out_ref[0, :HD] = (mixed / total).astype(jnp.bfloat16)
    level = best + jnp.log2(total)
    high = level.astype(jnp.bfloat16).astype(jnp.float32)
    rest = level - high
    middle = rest.astype(jnp.bfloat16).astype(jnp.float32)
    low = rest - middle
    row = lax.broadcasted_iota(jnp.int32, (16, ROWS), 0)
    stats = jnp.where(row == 0, high, jnp.where(row == 1, middle, jnp.where(row == 2, low, 0.0)))
    out_ref[0, HD:] = stats.astype(jnp.bfloat16)


def attend(q, qcode, own_kv, other_kv, kcode):
    groups = q.shape[0]
    keys = kcode.shape[0]
    return pl.pallas_call(
        attend_kernel,
        grid=(groups,),
        in_specs=[
            pl.BlockSpec((1, ROWS, HD), lambda i: (i, 0, 0)),
            pl.BlockSpec((1, 1, ROWS), lambda i: (i, 0, 0)),
            pl.BlockSpec(own_kv.shape, lambda i: (0, 0, 0)),
            pl.BlockSpec(other_kv.shape, lambda i: (0, 0, 0)),
            pl.BlockSpec((keys, 128), lambda i: (0, 0)),
        ],
        out_specs=pl.BlockSpec((1, PART_ROWS, ROWS), lambda i: (i, 0, 0)),
        out_shape=jax.ShapeDtypeStruct((groups, PART_ROWS, ROWS), jnp.bfloat16),
        scratch_shapes=[pltpu.VMEM((HD, keys), jnp.bfloat16)],
        compiler_params=pltpu.CompilerParams(vmem_limit_bytes=GRANT),
        name="attend",
    )(q, qcode, own_kv, other_kv, kcode)


def combine_kernel(part_ref, out_ref):
    groups = part_ref.shape[0]
    levels = []
    for j in range(groups):
        stats = part_ref[j, HD:].astype(jnp.float32)
        levels.append(stats[0:1] + stats[1:2] + stats[2:3])
    best = levels[0]
    for level in levels[1:]:
        best = jnp.maximum(best, level)
    total = jnp.zeros_like(best)
    mixed = jnp.zeros((HD, ROWS), jnp.float32)
    for j in range(groups):
        share = jnp.exp2(levels[j] - best)
        total = total + share
        mixed = mixed + share * part_ref[j, :HD].astype(jnp.float32)
    out_ref[...] = jnp.transpose(mixed / total).astype(jnp.bfloat16)


def combine(parts):
    return pl.pallas_call(
        combine_kernel,
        out_shape=jax.ShapeDtypeStruct((ROWS, HD), jnp.bfloat16),
        compiler_params=pltpu.CompilerParams(vmem_limit_bytes=GRANT),
        name="combine",
    )(parts)


def output_kernel(attended_ref, w_ref, out_ref):
    total = jnp.zeros(out_ref.shape, jnp.float32)
    for h in range(attended_ref.shape[0]):
        head_out = jnp.dot(attended_ref[h], w_ref[h], preferred_element_type=jnp.float32)
        total = total + head_out.astype(jnp.bfloat16).astype(jnp.float32)
    out_ref[...] = total.astype(jnp.bfloat16)


def output(attended, w):
    return pl.pallas_call(
        output_kernel,
        out_shape=jax.ShapeDtypeStruct((ROWS, w.shape[2]), jnp.bfloat16),
        compiler_params=pltpu.CompilerParams(vmem_limit_bytes=GRANT),
        name="output",
    )(attended, w)


def send_to_all(array, axis, count, groups=None):
    copies = jnp.broadcast_to(array[None], (count,) + array.shape)
    return lax.all_to_all(copies, axis, 0, 0, axis_index_groups=groups)


def make_on_device(n_seq, n_head):
    group = CORES * BLOCK_Z
    blocks = n_seq // group
    near = [
        [g * group + b * CORES + c for b in range(BLOCK_Z)] for g in range(blocks) for c in range(CORES)
    ]
    far = [[g * group + i for g in range(blocks)] for i in range(group)]
    swap = [(i, i ^ 1) for i in range(n_seq)]
    keys = CORES * blocks * ROWS

    def codes(span_order, frame_id, camera_id):
        code = (frame_id * 8 + camera_id).reshape(-1, SPAN)[span_order]
        code = code.reshape(blocks, BLOCK_Z, CORES, ROWS)
        place = lax.axis_index("seq")
        core = place % CORES
        query_code = lax.dynamic_index_in_dim(code, place // group, 0, keepdims=False)
        query_code = lax.dynamic_index_in_dim(query_code, core, 1, keepdims=False)
        key_code = lax.dynamic_index_in_dim(code, place // CORES % BLOCK_Z, 1, keepdims=False)
        own = lax.dynamic_index_in_dim(key_code, core, 1, keepdims=False)
        other = lax.dynamic_index_in_dim(key_code, 1 - core, 1, keepdims=False)
        key_code = jnp.concatenate([own, other]).reshape(-1, 1)
        return query_code[:, None, :], jnp.broadcast_to(key_code, (keys, 128))

    def on_device(tokens, norm_gain, w_qkv, w_out, span_order, frame_id, camera_id):
        columns = tokens.shape[1]
        gathered = send_to_all(tokens, "head", n_head)
        query_code, key_code = codes(span_order, frame_id, camera_id)
        w_split = w_out.reshape(HD, n_head, columns).transpose(1, 0, 2)
        gathered, w_split, query_code, key_code = lax.optimization_barrier(
            (gathered, w_split, query_code, key_code)
        )
        w_columns = lax.all_to_all(w_split, "head", 0, 0)
        queries, kv = project(gathered, norm_gain.reshape(1, D), w_qkv.transpose(1, 0, 2))
        all_queries = lax.all_gather(queries, "seq", axis_index_groups=near)
        all_queries, kv, w_columns = lax.optimization_barrier((all_queries, kv, w_columns))
        own_kv = send_to_all(kv, "seq", blocks, far)
        other_kv = lax.ppermute(own_kv, "seq", swap)
        parts = attend(all_queries, query_code, own_kv, other_kv, key_code)
        parts = lax.all_to_all(parts, "seq", 0, 0, axis_index_groups=near)
        attended = combine(parts)
        all_attended = send_to_all(attended, "head", n_head)
        return output(all_attended, w_columns)

    return on_device


def solution(mesh):
    placed = (P("seq", "head"), P(), P(None, None, "head"), P("head", None), P(), P(), P())
    return jax.shard_map(
        make_on_device(mesh.shape["seq"], mesh.shape["head"]),
        mesh=mesh,
        in_specs=placed,
        out_specs=P("seq", "head"),
        check_vma=False,
    )
```

```python
import jax
import jax.numpy as jnp
from jax import lax
from jax.experimental import pallas as pl
from jax.experimental.pallas import tpu as pltpu
from jax.sharding import PartitionSpec as P


D = 4096
HD = 128
ROWS = 256
SPAN = 128
CORES = 2
BLOCK_Z = 4
GRANT = 16 << 20
MASKED = -1e30
EPSILON = 1e-06
LOG2_E = 1.4426950408889634
SCALE = HD**-0.5 * LOG2_E
PART_ROWS = HD + 16


def project_kernel(x_ref, gain_ref, w_ref, q_ref, kv_ref, inv_ref, acc_ref):
    step = pl.program_id(0)
    blocks = x_ref.shape[0]
    per_step = blocks // pl.num_programs(0)

    @pl.when(step == 0)
    def _():
        total = jnp.zeros((ROWS, x_ref.shape[2]), jnp.float32)
        for j in range(blocks):
            piece = x_ref[j].astype(jnp.float32)
            total = total + piece * piece
        mean = jnp.sum(total, axis=1, keepdims=True) * (1.0 / D)
        inv_ref[...] = jnp.broadcast_to(lax.rsqrt(mean + EPSILON), inv_ref.shape)
        acc_ref[...] = jnp.zeros_like(acc_ref)

    width = x_ref.shape[2]
    inverse = jnp.concatenate([inv_ref[...]] * (width // 128), axis=1)
    sums = acc_ref[...]
    for i in range(per_step):
        piece = x_ref[step * per_step + i].astype(jnp.float32)
        gain = gain_ref[:, i * width : (i + 1) * width]
        normed = (piece * inverse * gain).astype(jnp.bfloat16)
        rows = slice(i * width, (i + 1) * width)
        weights = jnp.concatenate([w_ref[0, rows], w_ref[1, rows], w_ref[2, rows]], axis=1)
        sums = sums + jnp.dot(normed, weights, preferred_element_type=jnp.float32)
    acc_ref[...] = sums

    @pl.when(step == pl.num_programs(0) - 1)
    def _():
        done = sums.astype(jnp.bfloat16)
        q_ref[...] = done[:, :HD]
        for j in range(kv_ref.shape[0]):
            kv_ref[j] = done[:, HD:]


def project(x, gain, w, copies):
    blocks, _, width = x.shape
    steps = 4
    depth = D // steps
    return pl.pallas_call(
        project_kernel,
        grid=(steps,),
        in_specs=[
            pl.BlockSpec((blocks, ROWS, width), lambda s: (0, 0, 0)),
            pl.BlockSpec((1, depth), lambda s: (0, s)),
            pl.BlockSpec((3, depth, HD), lambda s: (0, s, 0)),
        ],
        out_specs=[
            pl.BlockSpec((ROWS, HD), lambda s: (0, 0)),
            pl.BlockSpec((copies, ROWS, 2 * HD), lambda s: (0, 0, 0)),
        ],
        out_shape=[
            jax.ShapeDtypeStruct((ROWS, HD), jnp.bfloat16),
            jax.ShapeDtypeStruct((copies, ROWS, 2 * HD), jnp.bfloat16),
        ],
        scratch_shapes=[
            pltpu.VMEM((ROWS, 128), jnp.float32),
            pltpu.VMEM((ROWS, 3 * HD), jnp.float32),
        ],
        compiler_params=pltpu.CompilerParams(vmem_limit_bytes=GRANT),
        name="project",
    )(x, gain, w)


def attend_kernel(q_ref, qcode_ref, own_ref, other_ref, kcode_ref, out_ref, vt_ref):
    count = own_ref.shape[0]

    @pl.when(pl.program_id(0) == 0)
    def _():
        for part, ref in enumerate((own_ref, other_ref)):
            for j in range(count):
                at = (part * count + j) * ROWS
                vt_ref[:, at : at + ROWS] = jnp.transpose(ref[j][:, HD:])

    qcode = qcode_ref[0]
    qbase = qcode & -8
    queries = q_ref[0]
    scores = []
    for part, ref in enumerate((own_ref, other_ref)):
        for j in range(count):
            at = (part * count + j) * ROWS
            raw = lax.dot_general(
                ref[j][:, :HD],
                queries,
                (((1,), (1,)), ((), ())),
                preferred_element_type=jnp.float32,
            )
            code = kcode_ref[at : at + ROWS, :]
            kcode = jnp.concatenate([code] * (ROWS // 128), axis=1)
            seen = (kcode < qbase) | (kcode == qcode)
            scores.append(jnp.where(seen, raw * SCALE, MASKED))
    scores = jnp.concatenate(scores, axis=0)
    best = jnp.max(scores, axis=0, keepdims=True)
    weights = jnp.exp2(scores - best)
    total = jnp.sum(weights, axis=0, keepdims=True)
    mixed = jnp.dot(vt_ref[...], weights.astype(jnp.bfloat16), preferred_element_type=jnp.float32)
    out_ref[0, :HD] = (mixed / total).astype(jnp.bfloat16)
    level = best + jnp.log2(total)
    high = level.astype(jnp.bfloat16).astype(jnp.float32)
    rest = level - high
    middle = rest.astype(jnp.bfloat16).astype(jnp.float32)
    low = rest - middle
    row = lax.broadcasted_iota(jnp.int32, (16, ROWS), 0)
    stats = jnp.where(row == 0, high, jnp.where(row == 1, middle, jnp.where(row == 2, low, 0.0)))
    out_ref[0, HD:] = stats.astype(jnp.bfloat16)


def attend(q, qcode, own_kv, other_kv, kcode):
    groups = q.shape[0]
    keys = kcode.shape[0]
    return pl.pallas_call(
        attend_kernel,
        grid=(groups,),
        in_specs=[
            pl.BlockSpec((1, ROWS, HD), lambda i: (i, 0, 0)),
            pl.BlockSpec((1, 1, ROWS), lambda i: (i, 0, 0)),
            pl.BlockSpec(own_kv.shape, lambda i: (0, 0, 0)),
            pl.BlockSpec(other_kv.shape, lambda i: (0, 0, 0)),
            pl.BlockSpec((keys, 128), lambda i: (0, 0)),
        ],
        out_specs=pl.BlockSpec((1, PART_ROWS, ROWS), lambda i: (i, 0, 0)),
        out_shape=jax.ShapeDtypeStruct((groups, PART_ROWS, ROWS), jnp.bfloat16),
        scratch_shapes=[pltpu.VMEM((HD, keys), jnp.bfloat16)],
        compiler_params=pltpu.CompilerParams(vmem_limit_bytes=GRANT),
        name="attend",
    )(q, qcode, own_kv, other_kv, kcode)


def combine_kernel(part_ref, out_ref):
    groups = part_ref.shape[0]
    levels = []
    for j in range(groups):
        stats = part_ref[j, HD:].astype(jnp.float32)
        levels.append(stats[0:1] + stats[1:2] + stats[2:3])
    best = levels[0]
    for level in levels[1:]:
        best = jnp.maximum(best, level)
    total = jnp.zeros_like(best)
    mixed = jnp.zeros((HD, ROWS), jnp.float32)
    for j in range(groups):
        share = jnp.exp2(levels[j] - best)
        total = total + share
        mixed = mixed + share * part_ref[j, :HD].astype(jnp.float32)
    attended = jnp.transpose(mixed / total).astype(jnp.bfloat16)
    for j in range(out_ref.shape[0]):
        out_ref[j] = attended


def combine(parts, copies):
    return pl.pallas_call(
        combine_kernel,
        out_shape=jax.ShapeDtypeStruct((copies, ROWS, HD), jnp.bfloat16),
        compiler_params=pltpu.CompilerParams(vmem_limit_bytes=GRANT),
        name="combine",
    )(parts)


def output_kernel(attended_ref, w_ref, out_ref):
    total = jnp.zeros(out_ref.shape, jnp.float32)
    for h in range(attended_ref.shape[0]):
        head_out = jnp.dot(attended_ref[h], w_ref[h], preferred_element_type=jnp.float32)
        total = total + head_out.astype(jnp.bfloat16).astype(jnp.float32)
    out_ref[...] = total.astype(jnp.bfloat16)


def output(attended, w):
    return pl.pallas_call(
        output_kernel,
        out_shape=jax.ShapeDtypeStruct((ROWS, w.shape[2]), jnp.bfloat16),
        compiler_params=pltpu.CompilerParams(vmem_limit_bytes=GRANT),
        name="output",
    )(attended, w)


def make_on_device(n_seq, n_head):
    group = CORES * BLOCK_Z
    blocks = n_seq // group
    near = [
        [g * group + b * CORES + c for b in range(BLOCK_Z)] for g in range(blocks) for c in range(CORES)
    ]
    far = [[g * group + i for g in range(blocks)] for i in range(group)]
    swap = [(i, i ^ 1) for i in range(n_seq)]
    keys = CORES * blocks * ROWS

    def codes(span_order, frame_id, camera_id):
        code = (frame_id * 8 + camera_id).reshape(-1, SPAN)[span_order]
        code = code.reshape(blocks, BLOCK_Z, CORES, ROWS)
        place = lax.axis_index("seq")
        core = place % CORES
        query_code = lax.dynamic_index_in_dim(code, place // group, 0, keepdims=False)
        query_code = lax.dynamic_index_in_dim(query_code, core, 1, keepdims=False)
        key_code = lax.dynamic_index_in_dim(code, place // CORES % BLOCK_Z, 1, keepdims=False)
        own = lax.dynamic_index_in_dim(key_code, core, 1, keepdims=False)
        other = lax.dynamic_index_in_dim(key_code, 1 - core, 1, keepdims=False)
        key_code = jnp.concatenate([own, other]).reshape(-1, 1)
        return query_code[:, None, :], jnp.broadcast_to(key_code, (keys, 128))

    def on_device(tokens, norm_gain, w_qkv, w_out, span_order, frame_id, camera_id):
        columns = tokens.shape[1]
        copies = jnp.broadcast_to(tokens[None], (n_head,) + tokens.shape)
        gathered = lax.all_to_all(copies, "head", 0, 0)
        query_code, key_code = codes(span_order, frame_id, camera_id)
        w_split = w_out.reshape(HD, n_head, columns).transpose(1, 0, 2)
        gathered, w_split, query_code, key_code = lax.optimization_barrier(
            (gathered, w_split, query_code, key_code)
        )
        w_columns = lax.all_to_all(w_split, "head", 0, 0)
        queries, kv = project(gathered, norm_gain.reshape(1, D), w_qkv.transpose(1, 0, 2), blocks)
        all_queries = lax.all_gather(queries, "seq", axis_index_groups=near)
        all_queries, kv, w_columns = lax.optimization_barrier((all_queries, kv, w_columns))
        own_kv = lax.all_to_all(kv, "seq", 0, 0, axis_index_groups=far)
        other_kv = lax.ppermute(own_kv, "seq", swap)
        parts = attend(all_queries, query_code, own_kv, other_kv, key_code)
        parts = lax.all_to_all(parts, "seq", 0, 0, axis_index_groups=near)
        attended = combine(parts, n_head)
        all_attended = lax.all_to_all(attended, "head", 0, 0)
        return output(all_attended, w_columns)

    return on_device


def solution(mesh):
    placed = (P("seq", "head"), P(), P(None, None, "head"), P("head", None), P(), P(), P())
    return jax.shard_map(
        make_on_device(mesh.shape["seq"], mesh.shape["head"]),
        mesh=mesh,
        in_specs=placed,
        out_specs=P("seq", "head"),
        check_vma=False,
    )
```

```python
import math

import jax
import jax.numpy as jnp
from jax import lax
from jax.experimental import pallas as pl
from jax.experimental.pallas import tpu as pltpu
from jax.sharding import PartitionSpec as P


D = 4096
HD = 128
ROWS = 256
SPAN = 128
CORES = 2
BLOCK_Z = 4
GRANT = 16 << 20
MASKED = -1e30
EPSILON = 1e-06
LOG2_E = 1.4426950408889634
SCALE = HD**-0.5 * LOG2_E
PART_ROWS = HD + 16


def project_kernel(x_ref, gain_ref, w_ref, q_ref, kv_ref, inv_ref, acc_ref):
    step = pl.program_id(0)
    blocks = x_ref.shape[0]
    per_step = blocks // pl.num_programs(0)

    @pl.when(step == 0)
    def _():
        total = jnp.zeros((ROWS, x_ref.shape[2]), jnp.float32)
        for j in range(blocks):
            piece = x_ref[j].astype(jnp.float32)
            total = total + piece * piece
        mean = jnp.sum(total, axis=1, keepdims=True) * (1.0 / D)
        inv_ref[...] = jnp.broadcast_to(lax.rsqrt(mean + EPSILON), inv_ref.shape)
        acc_ref[...] = jnp.zeros_like(acc_ref)

    width = x_ref.shape[2]
    inverse = jnp.concatenate([inv_ref[...]] * (width // 128), axis=1)
    sums = acc_ref[...]
    for i in range(per_step):
        piece = x_ref[step * per_step + i].astype(jnp.float32)
        gain = gain_ref[:, i * width : (i + 1) * width]
        normed = (piece * inverse * gain).astype(jnp.bfloat16)
        rows = slice(i * width, (i + 1) * width)
        weights = jnp.concatenate([w_ref[0, rows], w_ref[1, rows], w_ref[2, rows]], axis=1)
        sums = sums + jnp.dot(normed, weights, preferred_element_type=jnp.float32)
    acc_ref[...] = sums

    @pl.when(step == pl.num_programs(0) - 1)
    def _():
        done = sums.astype(jnp.bfloat16)
        q_ref[...] = done[:, :HD]
        for j in range(kv_ref.shape[0]):
            kv_ref[j] = done[:, HD:]


def project(x, gain, w, copies):
    blocks, _, width = x.shape
    steps = 4
    depth = D // steps
    return pl.pallas_call(
        project_kernel,
        grid=(steps,),
        in_specs=[
            pl.BlockSpec((blocks, ROWS, width), lambda s: (0, 0, 0)),
            pl.BlockSpec((1, depth), lambda s: (0, s)),
            pl.BlockSpec((3, depth, HD), lambda s: (0, s, 0)),
        ],
        out_specs=[
            pl.BlockSpec((ROWS, HD), lambda s: (0, 0)),
            pl.BlockSpec((copies, ROWS, 2 * HD), lambda s: (0, 0, 0)),
        ],
        out_shape=[
            jax.ShapeDtypeStruct((ROWS, HD), jnp.bfloat16),
            jax.ShapeDtypeStruct((copies, ROWS, 2 * HD), jnp.bfloat16),
        ],
        scratch_shapes=[
            pltpu.VMEM((ROWS, 128), jnp.float32),
            pltpu.VMEM((ROWS, 3 * HD), jnp.float32),
        ],
        compiler_params=pltpu.CompilerParams(vmem_limit_bytes=GRANT),
        name="project",
    )(x, gain, w)


def attend_kernel(q_ref, qcode_ref, own_ref, other_ref, kcode_ref, out_ref, vt_ref):
    count = own_ref.shape[0]

    @pl.when(pl.program_id(0) == 0)
    def _():
        for part, ref in enumerate((own_ref, other_ref)):
            for j in range(count):
                at = (part * count + j) * ROWS
                vt_ref[:, at : at + ROWS] = jnp.transpose(ref[j][:, HD:])

    qcode = qcode_ref[0]
    qbase = qcode & -8
    queries = q_ref[0]
    scores = []
    for part, ref in enumerate((own_ref, other_ref)):
        for j in range(count):
            at = (part * count + j) * ROWS
            raw = lax.dot_general(
                ref[j][:, :HD],
                queries,
                (((1,), (1,)), ((), ())),
                preferred_element_type=jnp.float32,
            )
            code = kcode_ref[at : at + ROWS, :]
            kcode = jnp.concatenate([code] * (ROWS // 128), axis=1)
            seen = (kcode < qbase) | (kcode == qcode)
            scores.append(jnp.where(seen, raw * SCALE, MASKED))
    scores = jnp.concatenate(scores, axis=0)
    best = jnp.max(scores, axis=0, keepdims=True)
    weights = jnp.exp2(scores - best)
    total = jnp.sum(weights, axis=0, keepdims=True)
    mixed = jnp.dot(vt_ref[...], weights.astype(jnp.bfloat16), preferred_element_type=jnp.float32)
    out_ref[0, :HD] = (mixed / total).astype(jnp.bfloat16)
    level = best + jnp.log2(total)
    high = level.astype(jnp.bfloat16).astype(jnp.float32)
    rest = level - high
    middle = rest.astype(jnp.bfloat16).astype(jnp.float32)
    low = rest - middle
    row = lax.broadcasted_iota(jnp.int32, (16, ROWS), 0)
    stats = jnp.where(row == 0, high, jnp.where(row == 1, middle, jnp.where(row == 2, low, 0.0)))
    out_ref[0, HD:] = stats.astype(jnp.bfloat16)


def attend(q, qcode, own_kv, other_kv, kcode):
    groups = q.shape[0]
    keys = kcode.shape[0]
    return pl.pallas_call(
        attend_kernel,
        grid=(groups,),
        in_specs=[
            pl.BlockSpec((1, ROWS, HD), lambda i: (i, 0, 0)),
            pl.BlockSpec((1, 1, ROWS), lambda i: (i, 0, 0)),
            pl.BlockSpec(own_kv.shape, lambda i: (0, 0, 0)),
            pl.BlockSpec(other_kv.shape, lambda i: (0, 0, 0)),
            pl.BlockSpec((keys, 128), lambda i: (0, 0)),
        ],
        out_specs=pl.BlockSpec((1, PART_ROWS, ROWS), lambda i: (i, 0, 0)),
        out_shape=jax.ShapeDtypeStruct((groups, PART_ROWS, ROWS), jnp.bfloat16),
        scratch_shapes=[pltpu.VMEM((HD, keys), jnp.bfloat16)],
        compiler_params=pltpu.CompilerParams(vmem_limit_bytes=GRANT),
        name="attend",
    )(q, qcode, own_kv, other_kv, kcode)


def combine_kernel(part_ref, out_ref):
    groups = part_ref.shape[0]
    levels = []
    for j in range(groups):
        stats = part_ref[j, HD:].astype(jnp.float32)
        levels.append(stats[0:1] + stats[1:2] + stats[2:3])
    best = levels[0]
    for level in levels[1:]:
        best = jnp.maximum(best, level)
    total = jnp.zeros_like(best)
    mixed = jnp.zeros((HD, ROWS), jnp.float32)
    for j in range(groups):
        share = jnp.exp2(levels[j] - best)
        total = total + share
        mixed = mixed + share * part_ref[j, :HD].astype(jnp.float32)
    attended = jnp.transpose(mixed / total).astype(jnp.bfloat16)
    for j in range(out_ref.shape[0]):
        out_ref[j] = attended


def combine(parts, copies):
    return pl.pallas_call(
        combine_kernel,
        out_shape=jax.ShapeDtypeStruct((copies, ROWS, HD), jnp.bfloat16),
        compiler_params=pltpu.CompilerParams(vmem_limit_bytes=GRANT),
        name="combine",
    )(parts)


def take_kernel(place_ref, w_ref, *out_refs):
    side = len(out_refs)
    width = out_refs[0].shape[2]
    for shift, out_ref in enumerate(out_refs):
        y = lax.rem(place_ref[1] + shift, side)
        for x in range(side):
            at = pl.multiple_of((x * side + y) * width, width)
            out_ref[x] = w_ref[:, pl.ds(at, width)]


def take(place, w, side):
    piece = jax.ShapeDtypeStruct((side, HD, w.shape[1] // side**2), w.dtype)
    return pl.pallas_call(
        take_kernel,
        in_specs=[
            pl.BlockSpec(memory_space=pltpu.SMEM),
            pl.BlockSpec(memory_space=pltpu.VMEM),
        ],
        out_shape=[piece] * side,
        compiler_params=pltpu.CompilerParams(vmem_limit_bytes=GRANT),
        name="take",
    )(place, w)


def turn_kernel(place_ref, *refs):
    side = len(refs) // 2
    for shift, out_ref in enumerate(refs[side:]):
        x = lax.rem(place_ref[0] + shift, side)
        for j in range(side):
            out_ref[j] = refs[j][x]


def turn(place, pieces):
    return pl.pallas_call(
        turn_kernel,
        in_specs=[pl.BlockSpec(memory_space=pltpu.SMEM)]
        + [pl.BlockSpec(memory_space=pltpu.VMEM)] * len(pieces),
        out_shape=[jax.ShapeDtypeStruct(p.shape, p.dtype) for p in pieces],
        compiler_params=pltpu.CompilerParams(vmem_limit_bytes=GRANT),
        name="turn",
    )(place, *pieces)


def output_kernel(place_ref, attended_ref, *refs):
    out_ref = refs[-1]
    side = len(refs) - 1
    total = jnp.zeros(out_ref.shape, jnp.float32)
    for k in range(side):
        for j in range(side):
            x = lax.rem(place_ref[0] + (side - k), side)
            y = lax.rem(place_ref[1] + (side - j), side)
            rows = attended_ref[x * side + y]
            head_out = jnp.dot(rows, refs[k][j], preferred_element_type=jnp.float32)
            total = total + head_out.astype(jnp.bfloat16).astype(jnp.float32)
    out_ref[...] = total.astype(jnp.bfloat16)


def output(place, attended, pieces):
    return pl.pallas_call(
        output_kernel,
        in_specs=[pl.BlockSpec(memory_space=pltpu.SMEM)]
        + [pl.BlockSpec(memory_space=pltpu.VMEM)] * (1 + len(pieces)),
        out_shape=jax.ShapeDtypeStruct((ROWS, pieces[0].shape[2]), jnp.bfloat16),
        compiler_params=pltpu.CompilerParams(vmem_limit_bytes=GRANT),
        name="output",
    )(place, attended, *pieces)


def make_on_device(n_seq, n_head):
    group = CORES * BLOCK_Z
    blocks = n_seq // group
    near = [
        [g * group + b * CORES + c for b in range(BLOCK_Z)] for g in range(blocks) for c in range(CORES)
    ]
    far = [[g * group + i for g in range(blocks)] for i in range(group)]
    swap = [(i, i ^ 1) for i in range(n_seq)]
    keys = CORES * blocks * ROWS

    def codes(span_order, frame_id, camera_id):
        code = (frame_id * 8 + camera_id).reshape(-1, SPAN)[span_order]
        code = code.reshape(blocks, BLOCK_Z, CORES, ROWS)
        place = lax.axis_index("seq")
        core = place % CORES
        query_code = lax.dynamic_index_in_dim(code, place // group, 0, keepdims=False)
        query_code = lax.dynamic_index_in_dim(query_code, core, 1, keepdims=False)
        key_code = lax.dynamic_index_in_dim(code, place // CORES % BLOCK_Z, 1, keepdims=False)
        own = lax.dynamic_index_in_dim(key_code, core, 1, keepdims=False)
        other = lax.dynamic_index_in_dim(key_code, 1 - core, 1, keepdims=False)
        key_code = jnp.concatenate([own, other]).reshape(-1, 1)
        return query_code[:, None, :], jnp.broadcast_to(key_code, (keys, 128))

    side = math.isqrt(n_head)
    along_x = [[(i, (i + k * side) % n_head) for i in range(n_head)] for k in range(side)]
    along_y = [
        [(i, i // side * side + (i + k) % side) for i in range(n_head)] for k in range(side)
    ]

    def on_device(tokens, norm_gain, w_qkv, w_out, span_order, frame_id, camera_id):
        head = lax.axis_index("head")
        place = jnp.stack([head // side, head % side]).astype(jnp.int32)
        copies = jnp.broadcast_to(tokens[None], (n_head,) + tokens.shape)
        gathered = lax.all_to_all(copies, "head", 0, 0)
        query_code, key_code = codes(span_order, frame_id, camera_id)
        taken = take(place, w_out, side)
        gathered, taken, query_code, key_code = lax.optimization_barrier(
            (gathered, taken, query_code, key_code)
        )
        queries, kv = project(gathered, norm_gain.reshape(1, D), w_qkv.transpose(1, 0, 2), blocks)
        all_queries = lax.all_gather(queries, "seq", axis_index_groups=near)
        all_queries, kv, taken = lax.optimization_barrier((all_queries, kv, taken))
        own_kv = lax.all_to_all(kv, "seq", 0, 0, axis_index_groups=far)
        taken = [taken[0]] + [lax.ppermute(taken[k], "head", along_y[k]) for k in range(1, side)]
        turned = turn(place, taken)
        w_columns = [turned[0]] + [
            lax.ppermute(turned[k], "head", along_x[k]) for k in range(1, side)
        ]
        other_kv = lax.ppermute(own_kv, "seq", swap)
        parts = attend(all_queries, query_code, own_kv, other_kv, key_code)
        parts = lax.all_to_all(parts, "seq", 0, 0, axis_index_groups=near)
        attended = combine(parts, n_head)
        all_attended = lax.all_to_all(attended, "head", 0, 0)
        return output(place, all_attended, w_columns)

    return on_device


def solution(mesh):
    placed = (P("seq", "head"), P(), P(None, None, "head"), P("head", None), P(), P(), P())
    return jax.shard_map(
        make_on_device(mesh.shape["seq"], mesh.shape["head"]),
        mesh=mesh,
        in_specs=placed,
        out_specs=P("seq", "head"),
        check_vma=False,
    )
```

```python
import math

import jax
import jax.numpy as jnp
from jax import lax
from jax.experimental import pallas as pl
from jax.experimental.pallas import tpu as pltpu
from jax.sharding import PartitionSpec as P


D = 4096
HD = 128
ROWS = 256
SPAN = 128
CORES = 2
BLOCK_Z = 4
GRANT = 16 << 20
MASKED = -1e30
EPSILON = 1e-06
LOG2_E = 1.4426950408889634
SCALE = HD**-0.5 * LOG2_E
PART_ROWS = HD + 16


def stage_kernel(w_ref, out_ref):
    out_ref[...] = w_ref[...]


def stage(w):
    rows = 1024
    spec = pl.BlockSpec((1, rows, HD), lambda i, j: (i, j, 0))
    return pl.pallas_call(
        stage_kernel,
        grid=(w.shape[0], w.shape[1] // rows),
        in_specs=[spec],
        out_specs=spec,
        out_shape=jax.ShapeDtypeStruct(w.shape, w.dtype),
        compiler_params=pltpu.CompilerParams(vmem_limit_bytes=4 << 20),
        name="stage",
    )(w)


def project_kernel(x_ref, gain_ref, w_ref, q_out, kv_out, q_ref, kv_ref, sems):
    blocks, _, width = x_ref.shape
    total = jnp.zeros((ROWS, width), jnp.float32)
    for j in range(blocks):
        piece = x_ref[j].astype(jnp.float32)
        total = total + piece * piece
    mean = jnp.sum(total, axis=1, keepdims=True) * (1.0 / D)
    inverse = jnp.broadcast_to(lax.rsqrt(mean + EPSILON), (ROWS, width))
    sums = jnp.zeros((ROWS, 3 * HD), jnp.float32)
    for j in range(blocks):
        cols = slice(j * width, (j + 1) * width)
        normed = (x_ref[j].astype(jnp.float32) * inverse * gain_ref[:, cols]).astype(jnp.bfloat16)
        weights = jnp.concatenate([w_ref[0, cols], w_ref[1, cols], w_ref[2, cols]], axis=1)
        sums = sums + jnp.dot(normed, weights, preferred_element_type=jnp.float32)
    done = sums.astype(jnp.bfloat16)
    q_ref[...] = done[:, :HD]
    kv_ref[...] = done[:, HD:]
    sends = [
        pltpu.make_async_copy(q_ref, q_out.at[j], sems.at[0, j]) for j in range(q_out.shape[0])
    ] + [
        pltpu.make_async_copy(kv_ref, kv_out.at[j], sems.at[1, j]) for j in range(kv_out.shape[0])
    ]
    for send in sends:
        send.start()
    for send in sends:
        send.wait()


def project(x, gain, w, q_copies, kv_copies):
    return pl.pallas_call(
        project_kernel,
        in_specs=[pl.BlockSpec(memory_space=pltpu.VMEM)] * 3,
        out_specs=[pl.BlockSpec(memory_space=pltpu.HBM)] * 2,
        out_shape=[
            jax.ShapeDtypeStruct((q_copies, ROWS, HD), jnp.bfloat16),
            jax.ShapeDtypeStruct((kv_copies, ROWS, 2 * HD), jnp.bfloat16),
        ],
        scratch_shapes=[
            pltpu.VMEM((ROWS, HD), jnp.bfloat16),
            pltpu.VMEM((ROWS, 2 * HD), jnp.bfloat16),
            pltpu.SemaphoreType.DMA((2, max(q_copies, kv_copies))),
        ],
        compiler_params=pltpu.CompilerParams(vmem_limit_bytes=GRANT),
        name="project",
    )(x, gain, w)


def attend_kernel(q_ref, qcode_ref, own_ref, other_ref, kcode_ref, out_ref, vt_ref):
    count = own_ref.shape[0]

    @pl.when(pl.program_id(0) == 0)
    def _():
        for part, ref in enumerate((own_ref, other_ref)):
            for j in range(count):
                at = (part * count + j) * ROWS
                vt_ref[:, at : at + ROWS] = jnp.transpose(ref[j][:, HD:])

    qcode = qcode_ref[0]
    qbase = qcode & -8
    queries = q_ref[0]
    scores = []
    for part, ref in enumerate((own_ref, other_ref)):
        for j in range(count):
            at = (part * count + j) * ROWS
            raw = lax.dot_general(
                ref[j][:, :HD],
                queries,
                (((1,), (1,)), ((), ())),
                preferred_element_type=jnp.float32,
            )
            code = kcode_ref[at : at + ROWS, :]
            kcode = jnp.concatenate([code] * (ROWS // 128), axis=1)
            seen = (kcode < qbase) | (kcode == qcode)
            scores.append(jnp.where(seen, raw * SCALE, MASKED))
    scores = jnp.concatenate(scores, axis=0)
    best = jnp.max(scores, axis=0, keepdims=True)
    weights = jnp.exp2(scores - best)
    total = jnp.sum(weights, axis=0, keepdims=True)
    mixed = jnp.dot(vt_ref[...], weights.astype(jnp.bfloat16), preferred_element_type=jnp.float32)
    out_ref[0, :HD] = (mixed / total).astype(jnp.bfloat16)
    level = best + jnp.log2(total)
    high = level.astype(jnp.bfloat16).astype(jnp.float32)
    rest = level - high
    middle = rest.astype(jnp.bfloat16).astype(jnp.float32)
    low = rest - middle
    row = lax.broadcasted_iota(jnp.int32, (16, ROWS), 0)
    stats = jnp.where(row == 0, high, jnp.where(row == 1, middle, jnp.where(row == 2, low, 0.0)))
    out_ref[0, HD:] = stats.astype(jnp.bfloat16)


def attend(q, qcode, own_kv, other_kv, kcode):
    groups = q.shape[0]
    keys = kcode.shape[0]
    return pl.pallas_call(
        attend_kernel,
        grid=(groups,),
        in_specs=[
            pl.BlockSpec((1, ROWS, HD), lambda i: (i, 0, 0)),
            pl.BlockSpec((1, 1, ROWS), lambda i: (i, 0, 0)),
            pl.BlockSpec(own_kv.shape, lambda i: (0, 0, 0)),
            pl.BlockSpec(other_kv.shape, lambda i: (0, 0, 0)),
            pl.BlockSpec((keys, 128), lambda i: (0, 0)),
        ],
        out_specs=pl.BlockSpec((1, PART_ROWS, ROWS), lambda i: (i, 0, 0)),
        out_shape=jax.ShapeDtypeStruct((groups, PART_ROWS, ROWS), jnp.bfloat16),
        scratch_shapes=[pltpu.VMEM((HD, keys), jnp.bfloat16)],
        compiler_params=pltpu.CompilerParams(vmem_limit_bytes=GRANT),
        name="attend",
    )(q, qcode, own_kv, other_kv, kcode)


def combine_kernel(part_ref, out_ref):
    groups = part_ref.shape[0]
    levels = []
    for j in range(groups):
        stats = part_ref[j, HD:].astype(jnp.float32)
        levels.append(stats[0:1] + stats[1:2] + stats[2:3])
    best = levels[0]
    for level in levels[1:]:
        best = jnp.maximum(best, level)
    total = jnp.zeros_like(best)
    mixed = jnp.zeros((HD, ROWS), jnp.float32)
    for j in range(groups):
        share = jnp.exp2(levels[j] - best)
        total = total + share
        mixed = mixed + share * part_ref[j, :HD].astype(jnp.float32)
    attended = jnp.transpose(mixed / total).astype(jnp.bfloat16)
    for j in range(out_ref.shape[0]):
        out_ref[j] = attended


def combine(parts, copies):
    return pl.pallas_call(
        combine_kernel,
        out_shape=jax.ShapeDtypeStruct((copies, ROWS, HD), jnp.bfloat16),
        compiler_params=pltpu.CompilerParams(vmem_limit_bytes=GRANT),
        name="combine",
    )(parts)


def take_kernel(place_ref, w_ref, *out_refs):
    side = len(out_refs)
    width = out_refs[0].shape[2]
    for shift, out_ref in enumerate(out_refs):
        y = lax.rem(place_ref[1] + shift, side)
        for x in range(side):
            at = pl.multiple_of((x * side + y) * width, width)
            out_ref[x] = w_ref[:, pl.ds(at, width)]


def take(place, w, side):
    piece = jax.ShapeDtypeStruct((side, HD, w.shape[1] // side**2), w.dtype)
    return pl.pallas_call(
        take_kernel,
        in_specs=[
            pl.BlockSpec(memory_space=pltpu.SMEM),
            pl.BlockSpec(memory_space=pltpu.VMEM),
        ],
        out_shape=[piece] * side,
        compiler_params=pltpu.CompilerParams(vmem_limit_bytes=GRANT),
        name="take",
    )(place, w)


def turn_kernel(place_ref, *refs):
    side = (len(refs) + 1) // 2
    for shift, out_ref in enumerate(refs[side:], 1):
        x = lax.rem(place_ref[0] + shift, side)
        for j in range(side):
            out_ref[j] = refs[j][x]


def turn(place, pieces):
    return pl.pallas_call(
        turn_kernel,
        in_specs=[pl.BlockSpec(memory_space=pltpu.SMEM)]
        + [pl.BlockSpec(memory_space=pltpu.VMEM)] * len(pieces),
        out_shape=[jax.ShapeDtypeStruct(p.shape, p.dtype) for p in pieces[1:]],
        compiler_params=pltpu.CompilerParams(vmem_limit_bytes=GRANT),
        name="turn",
    )(place, *pieces)


def output_kernel(place_ref, attended_ref, *refs):
    out_ref = refs[-1]
    side = len(refs) // 2
    taken, moved = refs[:side], refs[side:-1]
    total = jnp.zeros(out_ref.shape, jnp.float32)
    for k in range(side):
        for j in range(side):
            x = lax.rem(place_ref[0] + (side - k), side)
            y = lax.rem(place_ref[1] + (side - j), side)
            rows = attended_ref[x * side + y]
            w = taken[j][x] if k == 0 else moved[k - 1][j]
            head_out = jnp.dot(rows, w, preferred_element_type=jnp.float32)
            total = total + head_out.astype(jnp.bfloat16).astype(jnp.float32)
    out_ref[...] = total.astype(jnp.bfloat16)


def output(place, attended, taken, moved):
    return pl.pallas_call(
        output_kernel,
        in_specs=[pl.BlockSpec(memory_space=pltpu.SMEM)]
        + [pl.BlockSpec(memory_space=pltpu.VMEM)] * (1 + len(taken) + len(moved)),
        out_shape=jax.ShapeDtypeStruct((ROWS, taken[0].shape[2]), jnp.bfloat16),
        compiler_params=pltpu.CompilerParams(vmem_limit_bytes=GRANT),
        name="output",
    )(place, attended, *taken, *moved)


def make_on_device(n_seq, n_head):
    group = CORES * BLOCK_Z
    blocks = n_seq // group
    near = [
        [g * group + b * CORES + c for b in range(BLOCK_Z)] for g in range(blocks) for c in range(CORES)
    ]
    far = [[g * group + i for g in range(blocks)] for i in range(group)]
    swap = [(i, i ^ 1) for i in range(n_seq)]
    keys = CORES * blocks * ROWS

    def codes(span_order, frame_id, camera_id):
        code = (frame_id * 8 + camera_id).reshape(-1, SPAN)[span_order]
        code = code.reshape(blocks, BLOCK_Z, CORES, ROWS)
        place = lax.axis_index("seq")
        core = place % CORES
        query_code = lax.dynamic_index_in_dim(code, place // group, 0, keepdims=False)
        query_code = lax.dynamic_index_in_dim(query_code, core, 1, keepdims=False)
        key_code = lax.dynamic_index_in_dim(code, place // CORES % BLOCK_Z, 1, keepdims=False)
        own = lax.dynamic_index_in_dim(key_code, core, 1, keepdims=False)
        other = lax.dynamic_index_in_dim(key_code, 1 - core, 1, keepdims=False)
        key_code = jnp.concatenate([own, other]).reshape(-1, 1)
        return query_code[:, None, :], jnp.broadcast_to(key_code, (keys, 128))

    side = math.isqrt(n_head)
    along_x = [[(i, (i + k * side) % n_head) for i in range(n_head)] for k in range(side)]
    along_y = [
        [(i, i // side * side + (i + k) % side) for i in range(n_head)] for k in range(side)
    ]

    def on_device(tokens, norm_gain, w_qkv, w_out, span_order, frame_id, camera_id):
        head = lax.axis_index("head")
        place = jnp.stack([head // side, head % side]).astype(jnp.int32)
        copies = jnp.broadcast_to(tokens[None], (n_head,) + tokens.shape)
        gathered = lax.all_to_all(copies, "head", 0, 0)
        query_code, key_code = codes(span_order, frame_id, camera_id)
        taken = take(place, w_out, side)
        w_heads = stage(w_qkv.transpose(1, 0, 2))
        gathered, taken, w_heads, query_code, key_code = lax.optimization_barrier(
            (gathered, taken, w_heads, query_code, key_code)
        )
        queries, kv = project(gathered, norm_gain.reshape(1, D), w_heads, BLOCK_Z, blocks)
        all_queries = lax.all_to_all(queries, "seq", 0, 0, axis_index_groups=near)
        all_queries, kv, taken = lax.optimization_barrier((all_queries, kv, taken))
        own_kv = lax.all_to_all(kv, "seq", 0, 0, axis_index_groups=far)
        taken = [taken[0]] + [lax.ppermute(taken[k], "head", along_y[k]) for k in range(1, side)]
        turned = turn(place, taken)
        moved = [
            lax.ppermute(piece, "head", along_x[k]) for k, piece in enumerate(turned, 1)
        ]
        other_kv = lax.ppermute(own_kv, "seq", swap)
        parts = attend(all_queries, query_code, own_kv, other_kv, key_code)
        parts = lax.all_to_all(parts, "seq", 0, 0, axis_index_groups=near)
        attended = combine(parts, n_head)
        all_attended = lax.all_to_all(attended, "head", 0, 0)
        return output(place, all_attended, taken, moved)

    return on_device


def solution(mesh):
    placed = (P("seq", "head"), P(), P(None, None, "head"), P("head", None), P(), P(), P())
    return jax.shard_map(
        make_on_device(mesh.shape["seq"], mesh.shape["head"]),
        mesh=mesh,
        in_specs=placed,
        out_specs=P("seq", "head"),
        check_vma=False,
    )
```

```python
import math

import jax
import jax.numpy as jnp
from jax import lax
from jax.experimental import pallas as pl
from jax.experimental.pallas import tpu as pltpu
from jax.sharding import PartitionSpec as P


D = 4096
HD = 128
ROWS = 256
SPAN = 128
CORES = 2
BLOCK_Z = 4
GRANT = 16 << 20
MASKED = -1e30
EPSILON = 1e-06
LOG2_E = 1.4426950408889634
SCALE = HD**-0.5 * LOG2_E
PART_ROWS = HD + 16


def stage_kernel(w_ref, out_ref):
    out_ref[...] = w_ref[...]


def stage(w):
    rows = 1024
    spec = pl.BlockSpec((1, rows, HD), lambda i, j: (i, j, 0))
    return pl.pallas_call(
        stage_kernel,
        grid=(w.shape[0], w.shape[1] // rows),
        in_specs=[spec],
        out_specs=spec,
        out_shape=jax.ShapeDtypeStruct(w.shape, w.dtype),
        compiler_params=pltpu.CompilerParams(vmem_limit_bytes=4 << 20),
        name="stage",
    )(w)


def project_kernel(x_ref, gain_ref, w_ref, q_ref, kv_ref):
    blocks, _, width = x_ref.shape
    total = jnp.zeros((ROWS, width), jnp.float32)
    for j in range(blocks):
        piece = x_ref[j].astype(jnp.float32)
        total = total + piece * piece
    mean = jnp.sum(total, axis=1, keepdims=True) * (1.0 / D)
    inverse = jnp.broadcast_to(lax.rsqrt(mean + EPSILON), (ROWS, width))
    sums = jnp.zeros((ROWS, 3 * HD), jnp.float32)
    for j in range(blocks):
        cols = slice(j * width, (j + 1) * width)
        normed = (x_ref[j].astype(jnp.float32) * inverse * gain_ref[:, cols]).astype(jnp.bfloat16)
        weights = jnp.concatenate([w_ref[0, cols], w_ref[1, cols], w_ref[2, cols]], axis=1)
        sums = sums + jnp.dot(normed, weights, preferred_element_type=jnp.float32)
    done = sums.astype(jnp.bfloat16)
    q_ref[...] = done[:, :HD]
    for j in range(kv_ref.shape[0]):
        kv_ref[j] = done[:, HD:]


def project(x, gain, w, copies):
    return pl.pallas_call(
        project_kernel,
        in_specs=[pl.BlockSpec(memory_space=pltpu.VMEM)] * 3,
        out_specs=[pl.BlockSpec(memory_space=pltpu.VMEM)] * 2,
        out_shape=[
            jax.ShapeDtypeStruct((ROWS, HD), jnp.bfloat16),
            jax.ShapeDtypeStruct((copies, ROWS, 2 * HD), jnp.bfloat16),
        ],
        compiler_params=pltpu.CompilerParams(vmem_limit_bytes=GRANT),
        name="project",
    )(x, gain, w)


def attend_kernel(qcode_ref, kcode_ref, own_ref, other_ref, *refs):
    q_refs, out_ref, vt_ref, column_ref = refs[:-3], refs[-3], refs[-2], refs[-1]
    groups = len(q_refs)
    block = lax.rem(lax.div(lax.axis_index("seq"), CORES), groups)
    count = own_ref.shape[0]
    unit = jnp.where(lax.broadcasted_iota(jnp.int32, (16, 128), 0) == 0, 8.0, 1.0)
    column_ref[...] = lax.dot_general(
        kcode_ref[...],
        unit.astype(jnp.bfloat16),
        (((0,), (0,)), ((), ())),
        preferred_element_type=jnp.float32,
    )
    for part, ref in enumerate((own_ref, other_ref)):
        for j in range(count):
            at = (part * count + j) * ROWS
            vt_ref[:, at : at + ROWS] = jnp.transpose(ref[j][:, HD:])

    for shift, q_ref in enumerate(q_refs):
        member = lax.rem(block + (groups - shift), groups)
        qcode = qcode_ref[member]
        qbase = (qcode & -8).astype(jnp.float32)
        qcode = qcode.astype(jnp.float32)
        queries = q_ref[...]
        scores = []
        for part, ref in enumerate((own_ref, other_ref)):
            for j in range(count):
                at = (part * count + j) * ROWS
                raw = lax.dot_general(
                    ref[j][:, :HD],
                    queries,
                    (((1,), (1,)), ((), ())),
                    preferred_element_type=jnp.float32,
                )
                code = column_ref[at : at + ROWS, :]
                kcode = jnp.concatenate([code] * (ROWS // 128), axis=1)
                seen = (kcode < qbase) | (kcode == qcode)
                scores.append(jnp.where(seen, raw * SCALE, MASKED))
        scores = jnp.concatenate(scores, axis=0)
        best = jnp.max(scores, axis=0, keepdims=True)
        weights = jnp.exp2(scores - best)
        total = jnp.sum(weights, axis=0, keepdims=True)
        mixed = jnp.dot(
            vt_ref[...], weights.astype(jnp.bfloat16), preferred_element_type=jnp.float32
        )
        out_ref[member, :HD] = (mixed / total).astype(jnp.bfloat16)
        level = best + jnp.log2(total)
        high = level.astype(jnp.bfloat16).astype(jnp.float32)
        rest = level - high
        middle = rest.astype(jnp.bfloat16).astype(jnp.float32)
        low = rest - middle
        row = lax.broadcasted_iota(jnp.int32, (16, ROWS), 0)
        stats = jnp.where(
            row == 0, high, jnp.where(row == 1, middle, jnp.where(row == 2, low, 0.0))
        )
        out_ref[member, HD:] = stats.astype(jnp.bfloat16)


def attend(queries, qcode, own_kv, other_kv, kcode):
    groups = len(queries)
    keys = kcode.shape[1]
    return pl.pallas_call(
        attend_kernel,
        in_specs=[pl.BlockSpec(memory_space=pltpu.VMEM)] * (4 + groups),
        out_shape=jax.ShapeDtypeStruct((groups, PART_ROWS, ROWS), jnp.bfloat16),
        scratch_shapes=[
            pltpu.VMEM((HD, keys), jnp.bfloat16),
            pltpu.VMEM((keys, 128), jnp.float32),
        ],
        compiler_params=pltpu.CompilerParams(vmem_limit_bytes=GRANT),
        name="attend",
    )(qcode, kcode, own_kv, other_kv, *queries)


def combine_kernel(part_ref, out_ref):
    groups = part_ref.shape[0]
    levels = []
    for j in range(groups):
        stats = part_ref[j, HD:].astype(jnp.float32)
        levels.append(stats[0:1] + stats[1:2] + stats[2:3])
    best = levels[0]
    for level in levels[1:]:
        best = jnp.maximum(best, level)
    total = jnp.zeros_like(best)
    mixed = jnp.zeros((HD, ROWS), jnp.float32)
    for j in range(groups):
        share = jnp.exp2(levels[j] - best)
        total = total + share
        mixed = mixed + share * part_ref[j, :HD].astype(jnp.float32)
    attended = jnp.transpose(mixed / total).astype(jnp.bfloat16)
    for j in range(out_ref.shape[0]):
        out_ref[j] = attended


def combine(parts, copies):
    return pl.pallas_call(
        combine_kernel,
        out_shape=jax.ShapeDtypeStruct((copies, ROWS, HD), jnp.bfloat16),
        compiler_params=pltpu.CompilerParams(vmem_limit_bytes=GRANT),
        name="combine",
    )(parts)


def head_place(side):
    head = lax.axis_index("head")
    return lax.div(head, side), lax.rem(head, side)


def take_kernel(w_ref, *out_refs):
    side = len(out_refs)
    _, own_y = head_place(side)
    width = out_refs[0].shape[2]
    for shift, out_ref in enumerate(out_refs):
        y = lax.rem(own_y + shift, side)
        for x in range(side):
            at = pl.multiple_of((x * side + y) * width, width)
            out_ref[x] = w_ref[:, pl.ds(at, width)]


def take(w, side):
    piece = jax.ShapeDtypeStruct((side, HD, w.shape[1] // side**2), w.dtype)
    return pl.pallas_call(
        take_kernel,
        in_specs=[pl.BlockSpec(memory_space=pltpu.VMEM)],
        out_shape=[piece] * side,
        compiler_params=pltpu.CompilerParams(vmem_limit_bytes=GRANT),
        name="take",
    )(w)


def turn_kernel(*refs):
    side = (len(refs) + 1) // 2
    own_x, _ = head_place(side)
    for shift, out_ref in enumerate(refs[side:], 1):
        x = lax.rem(own_x + shift, side)
        for j in range(side):
            out_ref[j] = refs[j][x]


def turn(pieces):
    return pl.pallas_call(
        turn_kernel,
        in_specs=[pl.BlockSpec(memory_space=pltpu.VMEM)] * len(pieces),
        out_shape=[jax.ShapeDtypeStruct(p.shape, p.dtype) for p in pieces[1:]],
        compiler_params=pltpu.CompilerParams(vmem_limit_bytes=GRANT),
        name="turn",
    )(*pieces)


def output_kernel(attended_ref, *refs):
    out_ref = refs[-1]
    side = len(refs) // 2
    own_x, own_y = head_place(side)
    taken, moved = refs[:side], refs[side:-1]
    total = jnp.zeros(out_ref.shape, jnp.float32)
    for k in range(side):
        for j in range(side):
            x = lax.rem(own_x + (side - k), side)
            y = lax.rem(own_y + (side - j), side)
            rows = attended_ref[x * side + y]
            w = taken[j][x] if k == 0 else moved[k - 1][j]
            head_out = jnp.dot(rows, w, preferred_element_type=jnp.float32)
            total = total + head_out.astype(jnp.bfloat16).astype(jnp.float32)
    out_ref[...] = total.astype(jnp.bfloat16)


def output(attended, taken, moved):
    return pl.pallas_call(
        output_kernel,
        in_specs=[pl.BlockSpec(memory_space=pltpu.VMEM)] * (1 + len(taken) + len(moved)),
        out_shape=jax.ShapeDtypeStruct((ROWS, taken[0].shape[2]), jnp.bfloat16),
        compiler_params=pltpu.CompilerParams(vmem_limit_bytes=GRANT),
        name="output",
    )(attended, *taken, *moved)


def make_on_device(n_seq, n_head):
    group = CORES * BLOCK_Z
    blocks = n_seq // group
    near = [
        [g * group + b * CORES + c for b in range(BLOCK_Z)] for g in range(blocks) for c in range(CORES)
    ]
    far = [[g * group + i for g in range(blocks)] for i in range(group)]
    swap = [(i, i ^ 1) for i in range(n_seq)]
    keys = CORES * blocks * ROWS

    def codes(span_order, frame_id, camera_id):
        code = (frame_id * 8 + camera_id).reshape(-1, SPAN)[span_order]
        code = code.reshape(blocks, BLOCK_Z, CORES, ROWS)
        place = lax.axis_index("seq")
        core = place % CORES
        query_code = lax.dynamic_index_in_dim(code, place // group, 0, keepdims=False)
        query_code = lax.dynamic_index_in_dim(query_code, core, 1, keepdims=False)
        key_code = lax.dynamic_index_in_dim(code, place // CORES % BLOCK_Z, 1, keepdims=False)
        own = lax.dynamic_index_in_dim(key_code, core, 1, keepdims=False)
        other = lax.dynamic_index_in_dim(key_code, 1 - core, 1, keepdims=False)
        key_code = jnp.concatenate([own, other]).reshape(1, keys)
        row = lax.broadcasted_iota(jnp.int32, (16, keys), 0)
        pair = jnp.where(row == 0, key_code >> 3, jnp.where(row == 1, key_code & 7, 0))
        return query_code[:, None, :], pair.astype(jnp.bfloat16)

    side = math.isqrt(n_head)
    along_block = [
        [(i, i // group * group + (i + k * CORES) % group) for i in range(n_seq)]
        for k in range(BLOCK_Z)
    ]
    along_x = [[(i, (i + k * side) % n_head) for i in range(n_head)] for k in range(side)]
    along_y = [
        [(i, i // side * side + (i + k) % side) for i in range(n_head)] for k in range(side)
    ]

    def on_device(tokens, norm_gain, w_qkv, w_out, span_order, frame_id, camera_id):
        copies = jnp.broadcast_to(tokens[None], (n_head,) + tokens.shape)
        gathered = lax.all_to_all(copies, "head", 0, 0)
        query_code, key_code = codes(span_order, frame_id, camera_id)
        taken = take(w_out, side)
        w_heads = stage(w_qkv.transpose(1, 0, 2))
        gathered, taken, w_heads, query_code, key_code = lax.optimization_barrier(
            (gathered, taken, w_heads, query_code, key_code)
        )
        queries, kv = project(gathered, norm_gain.reshape(1, D), w_heads, blocks)
        own_kv = lax.all_to_all(kv, "seq", 0, 0, axis_index_groups=far)
        all_queries = [queries] + [
            lax.ppermute(queries, "seq", along_block[k]) for k in range(1, BLOCK_Z)
        ]
        taken = [taken[0]] + [lax.ppermute(taken[k], "head", along_y[k]) for k in range(1, side)]
        turned = turn(taken)
        moved = [
            lax.ppermute(piece, "head", along_x[k]) for k, piece in enumerate(turned, 1)
        ]
        other_kv = lax.ppermute(own_kv, "seq", swap)
        parts = attend(all_queries, query_code, own_kv, other_kv, key_code)
        parts = lax.all_to_all(parts, "seq", 0, 0, axis_index_groups=near)
        attended = combine(parts, n_head)
        all_attended = lax.all_to_all(attended, "head", 0, 0)
        return output(all_attended, taken, moved)

    return on_device


def solution(mesh):
    placed = (P("seq", "head"), P(), P(None, None, "head"), P("head", None), P(), P(), P())
    return jax.shard_map(
        make_on_device(mesh.shape["seq"], mesh.shape["head"]),
        mesh=mesh,
        in_specs=placed,
        out_specs=P("seq", "head"),
        check_vma=False,
    )
```

```python
import jax
import jax.numpy as jnp
from jax import lax
from jax.experimental import pallas as pl
from jax.experimental.pallas import tpu as pltpu
from jax.sharding import PartitionSpec as P


D = 4096
HD = 128
ROWS = 256
SPAN = 128
CORES = 2
BLOCK_Z = 4
GRANT = 16 << 20
MASKED = -1e30
EPSILON = 1e-06
LOG2_E = 1.4426950408889634
SCALE = HD**-0.5 * LOG2_E
PART_ROWS = HD + 16


def stage_kernel(w_ref, out_ref):
    out_ref[...] = w_ref[...]


def stage(w):
    rows = 1024
    spec = pl.BlockSpec((1, rows, HD), lambda i, j: (i, j, 0))
    return pl.pallas_call(
        stage_kernel,
        grid=(w.shape[0], w.shape[1] // rows),
        in_specs=[spec],
        out_specs=spec,
        out_shape=jax.ShapeDtypeStruct(w.shape, w.dtype),
        compiler_params=pltpu.CompilerParams(vmem_limit_bytes=4 << 20),
        name="stage",
    )(w)


def project_kernel(x_ref, gain_ref, w_ref, q_ref, kv_ref):
    blocks, _, width = x_ref.shape
    total = jnp.zeros((ROWS, width), jnp.float32)
    for j in range(blocks):
        piece = x_ref[j].astype(jnp.float32)
        total = total + piece * piece
    mean = jnp.sum(total, axis=1, keepdims=True) * (1.0 / D)
    inverse = jnp.broadcast_to(lax.rsqrt(mean + EPSILON), (ROWS, width))
    sums = jnp.zeros((ROWS, 3 * HD), jnp.float32)
    for j in range(blocks):
        cols = slice(j * width, (j + 1) * width)
        normed = (x_ref[j].astype(jnp.float32) * inverse * gain_ref[:, cols]).astype(jnp.bfloat16)
        weights = jnp.concatenate([w_ref[0, cols], w_ref[1, cols], w_ref[2, cols]], axis=1)
        sums = sums + jnp.dot(normed, weights, preferred_element_type=jnp.float32)
    done = sums.astype(jnp.bfloat16)
    q_ref[...] = done[:, :HD]
    kv_ref[...] = done[:, HD:]


def project(x, gain, w):
    return pl.pallas_call(
        project_kernel,
        in_specs=[pl.BlockSpec(memory_space=pltpu.VMEM)] * 3,
        out_specs=[pl.BlockSpec(memory_space=pltpu.VMEM)] * 2,
        out_shape=[
            jax.ShapeDtypeStruct((ROWS, HD), jnp.bfloat16),
            jax.ShapeDtypeStruct((ROWS, 2 * HD), jnp.bfloat16),
        ],
        compiler_params=pltpu.CompilerParams(vmem_limit_bytes=GRANT),
        name="project",
    )(x, gain, w)


def attend_kernel(qcode_ref, kcode_ref, other_ref, *refs):
    count = other_ref.shape[0]
    own_refs, q_refs = refs[:count], refs[count:-3]
    out_ref, vt_ref, column_ref = refs[-3:]
    groups = len(q_refs)
    far_block = lax.div(lax.axis_index("seq"), CORES * groups)
    block = lax.rem(lax.div(lax.axis_index("seq"), CORES), groups)
    pieces = list(own_refs) + [other_ref.at[j] for j in range(count)]
    unit = jnp.where(lax.broadcasted_iota(jnp.int32, (16, 128), 0) == 0, 8.0, 1.0)
    column_ref[...] = lax.dot_general(
        kcode_ref[...],
        unit.astype(jnp.bfloat16),
        (((0,), (0,)), ((), ())),
        preferred_element_type=jnp.float32,
    )
    for j, ref in enumerate(pieces):
        vt_ref[:, j * ROWS : (j + 1) * ROWS] = jnp.transpose(ref[:, HD:])

    for shift, q_ref in enumerate(q_refs):
        member = lax.rem(block + (groups - shift), groups)
        qcode = qcode_ref[member]
        qbase = (qcode & -8).astype(jnp.float32)
        qcode = qcode.astype(jnp.float32)
        queries = q_ref[...]
        scores = []
        for j, ref in enumerate(pieces):
            raw = lax.dot_general(
                ref[:, :HD],
                queries,
                (((1,), (1,)), ((), ())),
                preferred_element_type=jnp.float32,
            )
            source = lax.rem(far_block + (count - j % count), count)
            at = pl.multiple_of((j // count * count + source) * ROWS, ROWS)
            code = column_ref[pl.ds(at, ROWS), :]
            kcode = jnp.concatenate([code] * (ROWS // 128), axis=1)
            seen = (kcode < qbase) | (kcode == qcode)
            scores.append(jnp.where(seen, raw * SCALE, MASKED))
        scores = jnp.concatenate(scores, axis=0)
        best = jnp.max(scores, axis=0, keepdims=True)
        weights = jnp.exp2(scores - best)
        total = jnp.sum(weights, axis=0, keepdims=True)
        mixed = jnp.dot(
            vt_ref[...], weights.astype(jnp.bfloat16), preferred_element_type=jnp.float32
        )
        out_ref[member, :HD] = (mixed / total).astype(jnp.bfloat16)
        level = best + jnp.log2(total)
        high = level.astype(jnp.bfloat16).astype(jnp.float32)
        rest = level - high
        middle = rest.astype(jnp.bfloat16).astype(jnp.float32)
        low = rest - middle
        row = lax.broadcasted_iota(jnp.int32, (16, ROWS), 0)
        stats = jnp.where(
            row == 0, high, jnp.where(row == 1, middle, jnp.where(row == 2, low, 0.0))
        )
        out_ref[member, HD:] = stats.astype(jnp.bfloat16)


def attend(queries, qcode, own_kv, other_kv, kcode):
    groups = len(queries)
    keys = kcode.shape[1]
    return pl.pallas_call(
        attend_kernel,
        in_specs=[pl.BlockSpec(memory_space=pltpu.VMEM)] * (3 + len(own_kv) + groups),
        out_shape=jax.ShapeDtypeStruct((groups, PART_ROWS, ROWS), jnp.bfloat16),
        scratch_shapes=[
            pltpu.VMEM((HD, keys), jnp.bfloat16),
            pltpu.VMEM((keys, 128), jnp.float32),
        ],
        compiler_params=pltpu.CompilerParams(vmem_limit_bytes=GRANT),
        name="attend",
    )(qcode, kcode, other_kv, *own_kv, *queries)


def combine_kernel(part_ref, out_ref):
    groups = part_ref.shape[0]
    levels = []
    for j in range(groups):
        stats = part_ref[j, HD:].astype(jnp.float32)
        levels.append(stats[0:1] + stats[1:2] + stats[2:3])
    best = levels[0]
    for level in levels[1:]:
        best = jnp.maximum(best, level)
    total = jnp.zeros_like(best)
    mixed = jnp.zeros((HD, ROWS), jnp.float32)
    for j in range(groups):
        share = jnp.exp2(levels[j] - best)
        total = total + share
        mixed = mixed + share * part_ref[j, :HD].astype(jnp.float32)
    attended = jnp.transpose(mixed / total).astype(jnp.bfloat16)
    for j in range(out_ref.shape[0]):
        out_ref[j] = attended


def combine(parts, copies):
    return pl.pallas_call(
        combine_kernel,
        out_shape=jax.ShapeDtypeStruct((copies, ROWS, HD), jnp.bfloat16),
        compiler_params=pltpu.CompilerParams(vmem_limit_bytes=GRANT),
        name="combine",
    )(parts)


def split_kernel(w_ref, out_ref):
    parts, _, width = out_ref.shape
    for j in range(parts):
        out_ref[j] = w_ref[:, j * width : (j + 1) * width]


def split(w, parts):
    return pl.pallas_call(
        split_kernel,
        in_specs=[pl.BlockSpec(memory_space=pltpu.VMEM)],
        out_shape=jax.ShapeDtypeStruct((parts, HD, w.shape[1] // parts), w.dtype),
        compiler_params=pltpu.CompilerParams(vmem_limit_bytes=GRANT),
        name="split",
    )(w)


def output_kernel(attended_ref, w_ref, out_ref):
    total = jnp.zeros(out_ref.shape, jnp.float32)
    for h in range(attended_ref.shape[0]):
        head_out = jnp.dot(attended_ref[h], w_ref[h], preferred_element_type=jnp.float32)
        total = total + head_out.astype(jnp.bfloat16).astype(jnp.float32)
    out_ref[...] = total.astype(jnp.bfloat16)


def output(attended, w):
    return pl.pallas_call(
        output_kernel,
        in_specs=[pl.BlockSpec(memory_space=pltpu.VMEM)] * 2,
        out_shape=jax.ShapeDtypeStruct((ROWS, w.shape[2]), jnp.bfloat16),
        compiler_params=pltpu.CompilerParams(vmem_limit_bytes=GRANT),
        name="output",
    )(attended, w)


def make_on_device(n_seq, n_head):
    group = CORES * BLOCK_Z
    blocks = n_seq // group
    near = [
        [g * group + b * CORES + c for b in range(BLOCK_Z)] for g in range(blocks) for c in range(CORES)
    ]
    swap = [(i, i ^ 1) for i in range(n_seq)]
    keys = CORES * blocks * ROWS

    def codes(span_order, frame_id, camera_id):
        code = (frame_id * 8 + camera_id).reshape(-1, SPAN)[span_order]
        code = code.reshape(blocks, BLOCK_Z, CORES, ROWS)
        place = lax.axis_index("seq")
        core = place % CORES
        query_code = lax.dynamic_index_in_dim(code, place // group, 0, keepdims=False)
        query_code = lax.dynamic_index_in_dim(query_code, core, 1, keepdims=False)
        key_code = lax.dynamic_index_in_dim(code, place // CORES % BLOCK_Z, 1, keepdims=False)
        own = lax.dynamic_index_in_dim(key_code, core, 1, keepdims=False)
        other = lax.dynamic_index_in_dim(key_code, 1 - core, 1, keepdims=False)
        key_code = jnp.concatenate([own, other]).reshape(1, keys)
        row = lax.broadcasted_iota(jnp.int32, (16, keys), 0)
        pair = jnp.where(row == 0, key_code >> 3, jnp.where(row == 1, key_code & 7, 0))
        return query_code[:, None, :], pair.astype(jnp.bfloat16)

    along_block = [
        [(i, i // group * group + (i + k * CORES) % group) for i in range(n_seq)]
        for k in range(BLOCK_Z)
    ]
    across = [[(i, (i + k * group) % n_seq) for i in range(n_seq)] for k in range(blocks)]

    def on_device(tokens, norm_gain, w_qkv, w_out, span_order, frame_id, camera_id):
        copies = jnp.broadcast_to(tokens[None], (n_head,) + tokens.shape)
        gathered = lax.all_to_all(copies, "head", 0, 0)
        query_code, key_code = codes(span_order, frame_id, camera_id)
        w_split = split(w_out, n_head)
        w_heads = stage(w_qkv.transpose(1, 0, 2))
        gathered, w_split, w_heads, query_code, key_code = lax.optimization_barrier(
            (gathered, w_split, w_heads, query_code, key_code)
        )
        queries, kv = project(gathered, norm_gain.reshape(1, D), w_heads)
        own_kv = [kv] * blocks
        for k in (1, blocks - 1):
            own_kv[k] = lax.ppermute(kv, "seq", across[k])
        for k in range(2, blocks - 1):
            own_kv[k] = lax.ppermute(kv, "seq", across[k])
        all_queries = [queries] + [
            lax.ppermute(queries, "seq", along_block[k]) for k in range(1, BLOCK_Z)
        ]
        w_columns = lax.all_to_all(w_split, "head", 0, 0)
        other_kv = lax.ppermute(jnp.stack(own_kv), "seq", swap)
        parts = attend(all_queries, query_code, own_kv, other_kv, key_code)
        parts, w_columns = lax.optimization_barrier((parts, w_columns))
        parts = lax.all_to_all(parts, "seq", 0, 0, axis_index_groups=near)
        attended = combine(parts, n_head)
        all_attended = lax.all_to_all(attended, "head", 0, 0)
        return output(all_attended, w_columns)

    return on_device


def solution(mesh):
    placed = (P("seq", "head"), P(), P(None, None, "head"), P("head", None), P(), P(), P())
    return jax.shard_map(
        make_on_device(mesh.shape["seq"], mesh.shape["head"]),
        mesh=mesh,
        in_specs=placed,
        out_specs=P("seq", "head"),
        check_vma=False,
    )
```

```python
import jax
import jax.numpy as jnp
from jax import lax
from jax.experimental import pallas as pl
from jax.experimental.pallas import tpu as pltpu
from jax.sharding import PartitionSpec as P


D = 4096
HD = 128
ROWS = 256
SPAN = 128
CORES = 2
BLOCK_Z = 4
GRANT = 16 << 20
MASKED = -1e30
EPSILON = 1e-06
LOG2_E = 1.4426950408889634
SCALE = HD**-0.5 * LOG2_E
PART_ROWS = HD + 16


def spread_kernel(x_ref, out_ref, sems):
    sends = [
        pltpu.make_async_copy(x_ref, out_ref.at[j], sems.at[j]) for j in range(out_ref.shape[0])
    ]
    for send in sends:
        send.start()
    for send in sends:
        send.wait()


def spread(x, copies):
    return pl.pallas_call(
        spread_kernel,
        in_specs=[pl.BlockSpec(memory_space=pltpu.VMEM)],
        out_specs=pl.BlockSpec(memory_space=pltpu.HBM),
        out_shape=jax.ShapeDtypeStruct((copies,) + x.shape, x.dtype),
        scratch_shapes=[pltpu.SemaphoreType.DMA((copies,))],
        name="spread",
    )(x)


def stage_kernel(w_ref, out_ref):
    out_ref[...] = w_ref[...]


def stage(w):
    rows = 1024
    spec = pl.BlockSpec((1, rows, HD), lambda i, j: (i, j, 0))
    return pl.pallas_call(
        stage_kernel,
        grid=(w.shape[0], w.shape[1] // rows),
        in_specs=[spec],
        out_specs=spec,
        out_shape=jax.ShapeDtypeStruct(w.shape, w.dtype),
        compiler_params=pltpu.CompilerParams(vmem_limit_bytes=4 << 20),
        name="stage",
    )(w)


def project_kernel(x_ref, gain_ref, w_ref, q_ref, kv_ref, inv_ref, acc_ref):
    step = pl.program_id(0)
    blocks = x_ref.shape[0]
    per_step = blocks // pl.num_programs(0)

    @pl.when(step == 0)
    def _():
        total = jnp.zeros((ROWS, x_ref.shape[2]), jnp.float32)
        for j in range(blocks):
            piece = x_ref[j].astype(jnp.float32)
            total = total + piece * piece
        mean = jnp.sum(total, axis=1, keepdims=True) * (1.0 / D)
        inv_ref[...] = jnp.broadcast_to(lax.rsqrt(mean + EPSILON), inv_ref.shape)
        acc_ref[...] = jnp.zeros_like(acc_ref)

    width = x_ref.shape[2]
    inverse = jnp.concatenate([inv_ref[...]] * (width // 128), axis=1)
    sums = acc_ref[...]
    for i in range(per_step):
        piece = x_ref[step * per_step + i].astype(jnp.float32)
        gain = gain_ref[:, i * width : (i + 1) * width]
        normed = (piece * inverse * gain).astype(jnp.bfloat16)
        rows = slice(i * width, (i + 1) * width)
        weights = jnp.concatenate([w_ref[0, rows], w_ref[1, rows], w_ref[2, rows]], axis=1)
        sums = sums + jnp.dot(normed, weights, preferred_element_type=jnp.float32)
    acc_ref[...] = sums

    @pl.when(step == pl.num_programs(0) - 1)
    def _():
        done = sums.astype(jnp.bfloat16)
        q_ref[...] = done[:, :HD]
        kv_ref[...] = done[:, HD:]


def project(x, gain, w):
    blocks, _, width = x.shape
    steps = 4
    depth = D // steps
    return pl.pallas_call(
        project_kernel,
        grid=(steps,),
        in_specs=[
            pl.BlockSpec((blocks, ROWS, width), lambda s: (0, 0, 0)),
            pl.BlockSpec((1, depth), lambda s: (0, s)),
            pl.BlockSpec((3, depth, HD), lambda s: (0, s, 0)),
        ],
        out_specs=[
            pl.BlockSpec((ROWS, HD), lambda s: (0, 0)),
            pl.BlockSpec((ROWS, 2 * HD), lambda s: (0, 0)),
        ],
        out_shape=[
            jax.ShapeDtypeStruct((ROWS, HD), jnp.bfloat16),
            jax.ShapeDtypeStruct((ROWS, 2 * HD), jnp.bfloat16),
        ],
        scratch_shapes=[
            pltpu.VMEM((ROWS, 128), jnp.float32),
            pltpu.VMEM((ROWS, 3 * HD), jnp.float32),
        ],
        compiler_params=pltpu.CompilerParams(vmem_limit_bytes=GRANT),
        name="project",
    )(x, gain, w)


def attend_kernel(qcode_ref, kcode_ref, other_ref, *refs):
    count = other_ref.shape[0]
    own_refs = refs[:count]
    queries_ref, neighbour_ref, pair_ref = refs[count:-3]
    q_refs = [queries_ref, neighbour_ref, pair_ref.at[0], pair_ref.at[1]]
    out_ref, vt_ref, column_ref = refs[-3:]
    groups = len(q_refs)
    far_block = lax.div(lax.axis_index("seq"), CORES * groups)
    block = lax.rem(lax.div(lax.axis_index("seq"), CORES), groups)
    pieces = list(own_refs) + [other_ref.at[j] for j in range(count)]
    unit = jnp.where(lax.broadcasted_iota(jnp.int32, (16, 128), 0) == 0, 8.0, 1.0)
    column_ref[...] = lax.dot_general(
        kcode_ref[...],
        unit.astype(jnp.bfloat16),
        (((0,), (0,)), ((), ())),
        preferred_element_type=jnp.float32,
    )
    for j, ref in enumerate(pieces):
        vt_ref[:, j * ROWS : (j + 1) * ROWS] = jnp.transpose(ref[:, HD:])

    for shift, q_ref in enumerate(q_refs):
        member = lax.bitwise_xor(block, shift)
        qcode = qcode_ref[member]
        qbase = (qcode & -8).astype(jnp.float32)
        qcode = qcode.astype(jnp.float32)
        queries = q_ref[...]
        scores = []
        for j, ref in enumerate(pieces):
            raw = lax.dot_general(
                ref[:, :HD],
                queries,
                (((1,), (1,)), ((), ())),
                preferred_element_type=jnp.float32,
            )
            source = lax.rem(far_block + (count - j % count), count)
            at = pl.multiple_of((j // count * count + source) * ROWS, ROWS)
            code = column_ref[pl.ds(at, ROWS), :]
            kcode = jnp.concatenate([code] * (ROWS // 128), axis=1)
            seen = (kcode < qbase) | (kcode == qcode)
            scores.append(jnp.where(seen, raw * SCALE, MASKED))
        scores = jnp.concatenate(scores, axis=0)
        best = jnp.max(scores, axis=0, keepdims=True)
        weights = jnp.exp2(scores - best)
        total = jnp.sum(weights, axis=0, keepdims=True)
        mixed = jnp.dot(
            vt_ref[...], weights.astype(jnp.bfloat16), preferred_element_type=jnp.float32
        )
        out_ref[member, :HD] = (mixed / total).astype(jnp.bfloat16)
        level = best + jnp.log2(total)
        high = level.astype(jnp.bfloat16).astype(jnp.float32)
        rest = level - high
        middle = rest.astype(jnp.bfloat16).astype(jnp.float32)
        low = rest - middle
        row = lax.broadcasted_iota(jnp.int32, (16, ROWS), 0)
        stats = jnp.where(
            row == 0, high, jnp.where(row == 1, middle, jnp.where(row == 2, low, 0.0))
        )
        out_ref[member, HD:] = stats.astype(jnp.bfloat16)


def attend(queries, qcode, own_kv, other_kv, kcode):
    groups = qcode.shape[0]
    keys = kcode.shape[1]
    return pl.pallas_call(
        attend_kernel,
        in_specs=[pl.BlockSpec(memory_space=pltpu.VMEM)] * (3 + len(own_kv) + len(queries)),
        out_shape=jax.ShapeDtypeStruct((groups, PART_ROWS, ROWS), jnp.bfloat16),
        scratch_shapes=[
            pltpu.VMEM((HD, keys), jnp.bfloat16),
            pltpu.VMEM((keys, 128), jnp.float32),
        ],
        compiler_params=pltpu.CompilerParams(vmem_limit_bytes=GRANT),
        name="attend",
    )(qcode, kcode, other_kv, *own_kv, *queries)


def combine_kernel(part_ref, out_ref):
    groups = part_ref.shape[0]
    levels = []
    for j in range(groups):
        stats = part_ref[j, HD:].astype(jnp.float32)
        levels.append(stats[0:1] + stats[1:2] + stats[2:3])
    best = levels[0]
    for level in levels[1:]:
        best = jnp.maximum(best, level)
    total = jnp.zeros_like(best)
    mixed = jnp.zeros((HD, ROWS), jnp.float32)
    for j in range(groups):
        share = jnp.exp2(levels[j] - best)
        total = total + share
        mixed = mixed + share * part_ref[j, :HD].astype(jnp.float32)
    attended = jnp.transpose(mixed / total).astype(jnp.bfloat16)
    for j in range(out_ref.shape[0]):
        out_ref[j] = attended


def combine(parts, copies):
    return pl.pallas_call(
        combine_kernel,
        out_shape=jax.ShapeDtypeStruct((copies, ROWS, HD), jnp.bfloat16),
        compiler_params=pltpu.CompilerParams(vmem_limit_bytes=GRANT),
        name="combine",
    )(parts)


def split_kernel(w_ref, out_ref):
    parts, _, width = out_ref.shape
    for j in range(parts):
        out_ref[j] = w_ref[:, j * width : (j + 1) * width]


def split(w, parts):
    return pl.pallas_call(
        split_kernel,
        in_specs=[pl.BlockSpec(memory_space=pltpu.VMEM)],
        out_shape=jax.ShapeDtypeStruct((parts, HD, w.shape[1] // parts), w.dtype),
        compiler_params=pltpu.CompilerParams(vmem_limit_bytes=GRANT),
        name="split",
    )(w)


def output_kernel(attended_ref, w_ref, out_ref):
    total = jnp.zeros(out_ref.shape, jnp.float32)
    for h in range(attended_ref.shape[0]):
        head_out = jnp.dot(attended_ref[h], w_ref[h], preferred_element_type=jnp.float32)
        total = total + head_out.astype(jnp.bfloat16).astype(jnp.float32)
    out_ref[...] = total.astype(jnp.bfloat16)


def output(attended, w):
    return pl.pallas_call(
        output_kernel,
        in_specs=[pl.BlockSpec(memory_space=pltpu.VMEM)] * 2,
        out_shape=jax.ShapeDtypeStruct((ROWS, w.shape[2]), jnp.bfloat16),
        compiler_params=pltpu.CompilerParams(vmem_limit_bytes=GRANT),
        name="output",
    )(attended, w)


def make_on_device(n_seq, n_head):
    group = CORES * BLOCK_Z
    blocks = n_seq // group
    near = [
        [g * group + b * CORES + c for b in range(BLOCK_Z)] for g in range(blocks) for c in range(CORES)
    ]
    swap = [(i, i ^ 1) for i in range(n_seq)]
    keys = CORES * blocks * ROWS

    def codes(span_order, frame_id, camera_id):
        code = (frame_id * 8 + camera_id).reshape(-1, SPAN)[span_order]
        code = code.reshape(blocks, BLOCK_Z, CORES, ROWS)
        place = lax.axis_index("seq")
        core = place % CORES
        query_code = lax.dynamic_index_in_dim(code, place // group, 0, keepdims=False)
        query_code = lax.dynamic_index_in_dim(query_code, core, 1, keepdims=False)
        key_code = lax.dynamic_index_in_dim(code, place // CORES % BLOCK_Z, 1, keepdims=False)
        own = lax.dynamic_index_in_dim(key_code, core, 1, keepdims=False)
        other = lax.dynamic_index_in_dim(key_code, 1 - core, 1, keepdims=False)
        key_code = jnp.concatenate([own, other]).reshape(1, keys)
        row = lax.broadcasted_iota(jnp.int32, (16, keys), 0)
        pair = jnp.where(row == 0, key_code >> 3, jnp.where(row == 1, key_code & 7, 0))
        return query_code[:, None, :], pair.astype(jnp.bfloat16)

    flip_one = [(i, i ^ CORES) for i in range(n_seq)]
    flip_two = [(i, i ^ 2 * CORES) for i in range(n_seq)]
    across = [[(i, (i + k * group) % n_seq) for i in range(n_seq)] for k in range(blocks)]

    def on_device(tokens, norm_gain, w_qkv, w_out, span_order, frame_id, camera_id):
        gathered = lax.all_to_all(spread(tokens, n_head), "head", 0, 0)
        query_code, key_code = codes(span_order, frame_id, camera_id)
        w_split = split(w_out, n_head)
        w_heads = stage(w_qkv.transpose(1, 0, 2))
        gathered, w_split, w_heads, query_code, key_code = lax.optimization_barrier(
            (gathered, w_split, w_heads, query_code, key_code)
        )
        queries, kv = project(gathered, norm_gain.reshape(1, D), w_heads)
        own_kv = [kv] * blocks
        for k in (1, blocks - 1):
            own_kv[k] = lax.ppermute(kv, "seq", across[k])
        neighbour = lax.ppermute(queries, "seq", flip_one)
        for k in range(2, blocks - 1):
            own_kv[k] = lax.ppermute(kv, "seq", across[k])
        pair = lax.ppermute(jnp.stack([queries, neighbour]), "seq", flip_two)
        w_columns = lax.all_to_all(w_split, "head", 0, 0)
        other_kv = lax.ppermute(jnp.stack(own_kv), "seq", swap)
        parts = attend((queries, neighbour, pair), query_code, own_kv, other_kv, key_code)
        parts, w_columns = lax.optimization_barrier((parts, w_columns))
        parts = lax.all_to_all(parts, "seq", 0, 0, axis_index_groups=near)
        attended = combine(parts, n_head)
        all_attended = lax.all_to_all(attended, "head", 0, 0)
        return output(all_attended, w_columns)

    return on_device


def solution(mesh):
    placed = (P("seq", "head"), P(), P(None, None, "head"), P("head", None), P(), P(), P())
    return jax.shard_map(
        make_on_device(mesh.shape["seq"], mesh.shape["head"]),
        mesh=mesh,
        in_specs=placed,
        out_specs=P("seq", "head"),
        check_vma=False,
    )
```

```python
import jax
import jax.numpy as jnp
from jax import lax
from jax.experimental import pallas as pl
from jax.experimental.pallas import tpu as pltpu
from jax.sharding import PartitionSpec as P


D = 4096
HD = 128
ROWS = 256
SPAN = 128
CORES = 2
BLOCK_Z = 4
GRANT = 16 << 20
MASKED = -1e30
EPSILON = 1e-06
LOG2_E = 1.4426950408889634
SCALE = HD**-0.5 * LOG2_E
PART_ROWS = HD + 16


def stage_kernel(w_ref, out_ref):
    out_ref[...] = w_ref[...]


def stage(w):
    rows = 1024
    spec = pl.BlockSpec((1, rows, HD), lambda i, j: (i, j, 0))
    return pl.pallas_call(
        stage_kernel,
        grid=(w.shape[0], w.shape[1] // rows),
        in_specs=[spec],
        out_specs=spec,
        out_shape=jax.ShapeDtypeStruct(w.shape, w.dtype),
        compiler_params=pltpu.CompilerParams(vmem_limit_bytes=4 << 20),
        name="stage",
    )(w)


def project_kernel(x_ref, gain_ref, w_ref, q_ref, kv_ref):
    blocks, _, width = x_ref.shape
    total = jnp.zeros((ROWS, width), jnp.float32)
    for j in range(blocks):
        piece = x_ref[j].astype(jnp.float32)
        total = total + piece * piece
    mean = jnp.sum(total, axis=1, keepdims=True) * (1.0 / D)
    inverse = jnp.broadcast_to(lax.rsqrt(mean + EPSILON), (ROWS, width))
    sums = jnp.zeros((ROWS, 3 * HD), jnp.float32)
    for j in range(blocks):
        cols = slice(j * width, (j + 1) * width)
        normed = (x_ref[j].astype(jnp.float32) * inverse * gain_ref[:, cols]).astype(jnp.bfloat16)
        weights = jnp.concatenate([w_ref[0, cols], w_ref[1, cols], w_ref[2, cols]], axis=1)
        sums = sums + jnp.dot(normed, weights, preferred_element_type=jnp.float32)
    done = sums.astype(jnp.bfloat16)
    q_ref[...] = done[:, :HD]
    kv_ref[...] = done[:, HD:]


def project(x, gain, w):
    return pl.pallas_call(
        project_kernel,
        in_specs=[pl.BlockSpec(memory_space=pltpu.VMEM)] * 3,
        out_specs=[pl.BlockSpec(memory_space=pltpu.VMEM)] * 2,
        out_shape=[
            jax.ShapeDtypeStruct((ROWS, HD), jnp.bfloat16),
            jax.ShapeDtypeStruct((ROWS, 2 * HD), jnp.bfloat16),
        ],
        compiler_params=pltpu.CompilerParams(vmem_limit_bytes=GRANT),
        name="project",
    )(x, gain, w)


def visit(pieces, first, places, qcodes_ref, kcode_ref, q_refs, column_ref, vt_ref):
    unit = jnp.where(lax.broadcasted_iota(jnp.int32, (16, 128), 0) == 0, 8.0, 1.0)
    count = len(pieces)
    block, far_block = places
    groups = len(q_refs)
    column_ref[...] = lax.dot_general(
        kcode_ref[:, first : first + count * ROWS],
        unit.astype(jnp.bfloat16),
        (((0,), (0,)), ((), ())),
        preferred_element_type=jnp.float32,
    )
    for j, ref in enumerate(pieces):
        vt_ref[:, j * ROWS : (j + 1) * ROWS] = jnp.transpose(ref[:, HD:])

    for shift, q_ref in enumerate(q_refs):
        member = lax.rem(block + (groups - shift), groups)
        qcode = qcodes_ref[member]
        qbase = (qcode & -8).astype(jnp.float32)
        qcode = qcode.astype(jnp.float32)
        queries = q_ref[...]
        scores = []
        for j, ref in enumerate(pieces):
            raw = lax.dot_general(
                ref[:, :HD],
                queries,
                (((1,), (1,)), ((), ())),
                preferred_element_type=jnp.float32,
            )
            at = pl.multiple_of(lax.rem(far_block + (count - j), count) * ROWS, ROWS)
            code = column_ref[pl.ds(at, ROWS), :]
            kcode = jnp.concatenate([code] * (ROWS // 128), axis=1)
            seen = (kcode < qbase) | (kcode == qcode)
            scores.append(jnp.where(seen, raw * SCALE, MASKED))
        scores = jnp.concatenate(scores, axis=0)
        best = jnp.max(scores, axis=0, keepdims=True)
        yield shift, member, best, scores


def weigh(scores, best, vt_ref):
    weights = jnp.exp2(scores - best)
    total = jnp.sum(weights, axis=0, keepdims=True)
    mixed = jnp.dot(vt_ref[...], weights.astype(jnp.bfloat16), preferred_element_type=jnp.float32)
    return total, mixed


def places_of(groups):
    place = lax.axis_index("seq")
    return lax.rem(lax.div(place, CORES), groups), lax.div(place, CORES * groups)


def attend_own_kernel(qcode_ref, kcode_ref, *refs):
    groups = qcode_ref.shape[0]
    own_refs, q_refs = refs[:-groups - 4], refs[-groups - 4 : -4]
    mixed_ref, stat_ref, vt_ref, column_ref = refs[-4:]
    steps = visit(
        own_refs, 0, places_of(groups), qcode_ref, kcode_ref, q_refs, column_ref, vt_ref
    )
    for shift, _, best, scores in steps:
        total, mixed = weigh(scores, best, vt_ref)
        mixed_ref[shift] = mixed
        stat_ref[shift, 0:1] = best
        stat_ref[shift, 1:2] = total


def attend_other_kernel(qcode_ref, kcode_ref, other_ref, own_mixed_ref, own_stat_ref, *refs):
    groups = qcode_ref.shape[0]
    q_refs = refs[:groups]
    out_ref, vt_ref, column_ref = refs[groups:]
    count = other_ref.shape[0]
    pieces = [other_ref.at[j] for j in range(count)]
    steps = visit(
        pieces,
        count * ROWS,
        places_of(groups),
        qcode_ref,
        kcode_ref,
        q_refs,
        column_ref,
        vt_ref,
    )
    for shift, member, best, scores in steps:
        own_best = own_stat_ref[shift, 0:1]
        best = jnp.maximum(best, own_best)
        total, mixed = weigh(scores, best, vt_ref)
        factor = jnp.exp2(own_best - best)
        total = total + factor * own_stat_ref[shift, 1:2]
        mixed = mixed + factor * own_mixed_ref[shift]
        out_ref[member, :HD] = (mixed / total).astype(jnp.bfloat16)
        level = best + jnp.log2(total)
        high = level.astype(jnp.bfloat16).astype(jnp.float32)
        rest = level - high
        middle = rest.astype(jnp.bfloat16).astype(jnp.float32)
        low = rest - middle
        row = lax.broadcasted_iota(jnp.int32, (16, ROWS), 0)
        stats = jnp.where(
            row == 0, high, jnp.where(row == 1, middle, jnp.where(row == 2, low, 0.0))
        )
        out_ref[member, HD:] = stats.astype(jnp.bfloat16)


def attend_own(queries, qcode, own_kv, kcode):
    groups = len(queries)
    keys = len(own_kv) * ROWS
    return pl.pallas_call(
        attend_own_kernel,
        in_specs=[pl.BlockSpec(memory_space=pltpu.VMEM)] * (2 + len(own_kv) + groups),
        out_shape=[
            jax.ShapeDtypeStruct((groups, HD, ROWS), jnp.float32),
            jax.ShapeDtypeStruct((groups, 8, ROWS), jnp.float32),
        ],
        scratch_shapes=[
            pltpu.VMEM((HD, keys), jnp.bfloat16),
            pltpu.VMEM((keys, 128), jnp.float32),
        ],
        compiler_params=pltpu.CompilerParams(vmem_limit_bytes=GRANT),
        name="attend_own",
    )(qcode, kcode, *own_kv, *queries)


def attend_other(queries, qcode, other_kv, kcode, own_mixed, own_stat):
    groups = len(queries)
    keys = other_kv.shape[0] * ROWS
    return pl.pallas_call(
        attend_other_kernel,
        in_specs=[pl.BlockSpec(memory_space=pltpu.VMEM)] * (5 + groups),
        out_shape=jax.ShapeDtypeStruct((groups, PART_ROWS, ROWS), jnp.bfloat16),
        scratch_shapes=[
            pltpu.VMEM((HD, keys), jnp.bfloat16),
            pltpu.VMEM((keys, 128), jnp.float32),
        ],
        compiler_params=pltpu.CompilerParams(vmem_limit_bytes=GRANT),
        name="attend_other",
    )(qcode, kcode, other_kv, own_mixed, own_stat, *queries)


def combine_kernel(part_ref, out_ref):
    groups = part_ref.shape[0]
    levels = []
    for j in range(groups):
        stats = part_ref[j, HD:].astype(jnp.float32)
        levels.append(stats[0:1] + stats[1:2] + stats[2:3])
    best = levels[0]
    for level in levels[1:]:
        best = jnp.maximum(best, level)
    total = jnp.zeros_like(best)
    mixed = jnp.zeros((HD, ROWS), jnp.float32)
    for j in range(groups):
        share = jnp.exp2(levels[j] - best)
        total = total + share
        mixed = mixed + share * part_ref[j, :HD].astype(jnp.float32)
    attended = jnp.transpose(mixed / total).astype(jnp.bfloat16)
    for j in range(out_ref.shape[0]):
        out_ref[j] = attended


def combine(parts, copies):
    return pl.pallas_call(
        combine_kernel,
        out_shape=jax.ShapeDtypeStruct((copies, ROWS, HD), jnp.bfloat16),
        compiler_params=pltpu.CompilerParams(vmem_limit_bytes=GRANT),
        name="combine",
    )(parts)


def split_kernel(w_ref, out_ref):
    parts, _, width = out_ref.shape
    for j in range(parts):
        out_ref[j] = w_ref[:, j * width : (j + 1) * width]


def split(w, parts):
    return pl.pallas_call(
        split_kernel,
        in_specs=[pl.BlockSpec(memory_space=pltpu.VMEM)],
        out_shape=jax.ShapeDtypeStruct((parts, HD, w.shape[1] // parts), w.dtype),
        compiler_params=pltpu.CompilerParams(vmem_limit_bytes=GRANT),
        name="split",
    )(w)


def output_kernel(attended_ref, w_ref, out_ref):
    total = jnp.zeros(out_ref.shape, jnp.float32)
    for h in range(attended_ref.shape[0]):
        head_out = jnp.dot(attended_ref[h], w_ref[h], preferred_element_type=jnp.float32)
        total = total + head_out.astype(jnp.bfloat16).astype(jnp.float32)
    out_ref[...] = total.astype(jnp.bfloat16)


def output(attended, w):
    return pl.pallas_call(
        output_kernel,
        in_specs=[pl.BlockSpec(memory_space=pltpu.VMEM)] * 2,
        out_shape=jax.ShapeDtypeStruct((ROWS, w.shape[2]), jnp.bfloat16),
        compiler_params=pltpu.CompilerParams(vmem_limit_bytes=GRANT),
        name="output",
    )(attended, w)


def make_on_device(n_seq, n_head):
    group = CORES * BLOCK_Z
    blocks = n_seq // group
    near = [
        [g * group + b * CORES + c for b in range(BLOCK_Z)] for g in range(blocks) for c in range(CORES)
    ]
    swap = [(i, i ^ 1) for i in range(n_seq)]
    keys = CORES * blocks * ROWS

    def codes(span_order, frame_id, camera_id):
        code = (frame_id * 8 + camera_id).reshape(-1, SPAN)[span_order]
        code = code.reshape(blocks, BLOCK_Z, CORES, ROWS)
        place = lax.axis_index("seq")
        core = place % CORES
        query_code = lax.dynamic_index_in_dim(code, place // group, 0, keepdims=False)
        query_code = lax.dynamic_index_in_dim(query_code, core, 1, keepdims=False)
        key_code = lax.dynamic_index_in_dim(code, place // CORES % BLOCK_Z, 1, keepdims=False)
        own = lax.dynamic_index_in_dim(key_code, core, 1, keepdims=False)
        other = lax.dynamic_index_in_dim(key_code, 1 - core, 1, keepdims=False)
        key_code = jnp.concatenate([own, other]).reshape(1, keys)
        row = lax.broadcasted_iota(jnp.int32, (16, keys), 0)
        pair = jnp.where(row == 0, key_code >> 3, jnp.where(row == 1, key_code & 7, 0))
        return query_code[:, None, :], pair.astype(jnp.bfloat16)

    along_block = [
        [(i, i // group * group + (i + k * CORES) % group) for i in range(n_seq)]
        for k in range(BLOCK_Z)
    ]
    across = [[(i, (i + k * group) % n_seq) for i in range(n_seq)] for k in range(blocks)]

    def on_device(tokens, norm_gain, w_qkv, w_out, span_order, frame_id, camera_id):
        copies = jnp.broadcast_to(tokens[None], (n_head,) + tokens.shape)
        gathered = lax.all_to_all(copies, "head", 0, 0)
        query_code, key_code = codes(span_order, frame_id, camera_id)
        w_split = split(w_out, n_head)
        w_heads = stage(w_qkv.transpose(1, 0, 2))
        gathered, w_split, w_heads, query_code, key_code = lax.optimization_barrier(
            (gathered, w_split, w_heads, query_code, key_code)
        )
        queries, kv = project(gathered, norm_gain.reshape(1, D), w_heads)
        own_kv = [kv] * blocks
        for k in (1, blocks - 1):
            own_kv[k] = lax.ppermute(kv, "seq", across[k])
        for k in range(2, blocks - 1):
            own_kv[k] = lax.ppermute(kv, "seq", across[k])
        all_queries = [queries] + [
            lax.ppermute(queries, "seq", along_block[k]) for k in range(1, BLOCK_Z)
        ]
        w_columns = lax.all_to_all(w_split, "head", 0, 0)
        other_kv = lax.ppermute(jnp.stack(own_kv), "seq", swap)
        own_mixed, own_stat = attend_own(all_queries, query_code, own_kv, key_code)
        parts = attend_other(
            all_queries, query_code, other_kv, key_code, own_mixed, own_stat
        )
        parts, w_columns = lax.optimization_barrier((parts, w_columns))
        parts = lax.all_to_all(parts, "seq", 0, 0, axis_index_groups=near)
        attended = combine(parts, n_head)
        all_attended = lax.all_to_all(attended, "head", 0, 0)
        return output(all_attended, w_columns)

    return on_device


def solution(mesh):
    placed = (P("seq", "head"), P(), P(None, None, "head"), P("head", None), P(), P(), P())
    return jax.shard_map(
        make_on_device(mesh.shape["seq"], mesh.shape["head"]),
        mesh=mesh,
        in_specs=placed,
        out_specs=P("seq", "head"),
        check_vma=False,
    )
```

```python
import jax
import jax.numpy as jnp
from jax import lax
from jax.experimental import pallas as pl
from jax.experimental.pallas import tpu as pltpu
from jax.sharding import PartitionSpec as P


D = 4096
HD = 128
ROWS = 256
SPAN = 128
CORES = 2
BLOCK_Z = 4
GRANT = 16 << 20
MASKED = -1e30
EPSILON = 1e-06
LOG2_E = 1.4426950408889634
SCALE = HD**-0.5 * LOG2_E
PART_ROWS = HD + 16


def stage_kernel(w_ref, out_ref):
    out_ref[...] = w_ref[...]


def stage(w):
    rows = 1024
    spec = pl.BlockSpec((1, rows, HD), lambda i, j: (i, j, 0))
    return pl.pallas_call(
        stage_kernel,
        grid=(w.shape[0], w.shape[1] // rows),
        in_specs=[spec],
        out_specs=spec,
        out_shape=jax.ShapeDtypeStruct(w.shape, w.dtype),
        compiler_params=pltpu.CompilerParams(vmem_limit_bytes=4 << 20),
        name="stage",
    )(w)


def project_kernel(x_ref, gain_ref, w_ref, q_ref, kv_ref):
    blocks, _, width = x_ref.shape
    total = jnp.zeros((ROWS, width), jnp.float32)
    for j in range(blocks):
        piece = x_ref[j].astype(jnp.float32)
        total = total + piece * piece
    mean = jnp.sum(total, axis=1, keepdims=True) * (1.0 / D)
    inverse = jnp.broadcast_to(lax.rsqrt(mean + EPSILON), (ROWS, width))
    sums = jnp.zeros((ROWS, 3 * HD), jnp.float32)
    for j in range(blocks):
        cols = slice(j * width, (j + 1) * width)
        normed = (x_ref[j].astype(jnp.float32) * inverse * gain_ref[:, cols]).astype(jnp.bfloat16)
        weights = jnp.concatenate([w_ref[0, cols], w_ref[1, cols], w_ref[2, cols]], axis=1)
        sums = sums + jnp.dot(normed, weights, preferred_element_type=jnp.float32)
    done = sums.astype(jnp.bfloat16)
    q_ref[...] = done[:, :HD]
    kv_ref[...] = done[:, HD:]


def project(x, gain, w):
    return pl.pallas_call(
        project_kernel,
        in_specs=[pl.BlockSpec(memory_space=pltpu.VMEM)] * 3,
        out_specs=[pl.BlockSpec(memory_space=pltpu.VMEM)] * 2,
        out_shape=[
            jax.ShapeDtypeStruct((ROWS, HD), jnp.bfloat16),
            jax.ShapeDtypeStruct((ROWS, 2 * HD), jnp.bfloat16),
        ],
        compiler_params=pltpu.CompilerParams(vmem_limit_bytes=GRANT),
        name="project",
    )(x, gain, w)


def visit(pieces, first, places, qcodes_ref, kcode_ref, q_refs, column_ref, vt_ref):
    unit = jnp.where(lax.broadcasted_iota(jnp.int32, (16, 128), 0) == 0, 8.0, 1.0)
    count = len(pieces)
    block, far_block = places
    groups = len(q_refs)
    column_ref[...] = lax.dot_general(
        kcode_ref[:, first : first + count * ROWS],
        unit.astype(jnp.bfloat16),
        (((0,), (0,)), ((), ())),
        preferred_element_type=jnp.float32,
    )
    for j, ref in enumerate(pieces):
        vt_ref[:, j * ROWS : (j + 1) * ROWS] = jnp.transpose(ref[:, HD:])

    for shift, q_ref in enumerate(q_refs):
        member = lax.rem(block + (groups - shift), groups)
        qcode = qcodes_ref[member]
        qbase = (qcode & -8).astype(jnp.float32)
        qcode = qcode.astype(jnp.float32)
        queries = q_ref[...]
        scores = []
        for j, ref in enumerate(pieces):
            raw = lax.dot_general(
                ref[:, :HD],
                queries,
                (((1,), (1,)), ((), ())),
                preferred_element_type=jnp.float32,
            )
            at = pl.multiple_of(lax.rem(far_block + (count - j), count) * ROWS, ROWS)
            code = column_ref[pl.ds(at, ROWS), :]
            kcode = jnp.concatenate([code] * (ROWS // 128), axis=1)
            seen = (kcode < qbase) | (kcode == qcode)
            scores.append(jnp.where(seen, raw * SCALE, MASKED))
        scores = jnp.concatenate(scores, axis=0)
        best = jnp.max(scores, axis=0, keepdims=True)
        yield shift, member, best, scores


def weigh(scores, best, vt_ref):
    weights = jnp.exp2(scores - best)
    total = jnp.sum(weights, axis=0, keepdims=True)
    mixed = jnp.dot(vt_ref[...], weights.astype(jnp.bfloat16), preferred_element_type=jnp.float32)
    return total, mixed


def places_of(groups):
    place = lax.axis_index("seq")
    return lax.rem(lax.div(place, CORES), groups), lax.div(place, CORES * groups)


def attend_own_kernel(qcode_ref, kcode_ref, *refs):
    groups = qcode_ref.shape[0]
    own_refs, q_refs = refs[:-groups - 4], refs[-groups - 4 : -4]
    mixed_ref, stat_ref, vt_ref, column_ref = refs[-4:]
    steps = visit(
        own_refs, 0, places_of(groups), qcode_ref, kcode_ref, q_refs, column_ref, vt_ref
    )
    for shift, _, best, scores in steps:
        total, mixed = weigh(scores, best, vt_ref)
        mixed_ref[shift] = mixed
        stat_ref[shift, 0:1] = best
        stat_ref[shift, 1:2] = total


def attend_other_kernel(qcode_ref, kcode_ref, other_ref, own_mixed_ref, own_stat_ref, *refs):
    groups = qcode_ref.shape[0]
    q_refs = refs[:groups]
    out_ref, vt_ref, column_ref = refs[groups:]
    count = other_ref.shape[0]
    pieces = [other_ref.at[j] for j in range(count)]
    steps = visit(
        pieces,
        count * ROWS,
        places_of(groups),
        qcode_ref,
        kcode_ref,
        q_refs,
        column_ref,
        vt_ref,
    )
    for shift, member, best, scores in steps:
        own_best = own_stat_ref[shift, 0:1]
        best = jnp.maximum(best, own_best)
        total, mixed = weigh(scores, best, vt_ref)
        factor = jnp.exp2(own_best - best)
        total = total + factor * own_stat_ref[shift, 1:2]
        mixed = mixed + factor * own_mixed_ref[shift]
        out_ref[member, :HD] = (mixed / total).astype(jnp.bfloat16)
        level = best + jnp.log2(total)
        high = level.astype(jnp.bfloat16).astype(jnp.float32)
        rest = level - high
        middle = rest.astype(jnp.bfloat16).astype(jnp.float32)
        low = rest - middle
        row = lax.broadcasted_iota(jnp.int32, (16, ROWS), 0)
        stats = jnp.where(
            row == 0, high, jnp.where(row == 1, middle, jnp.where(row == 2, low, 0.0))
        )
        out_ref[member, HD:] = stats.astype(jnp.bfloat16)


def attend_own(queries, qcode, own_kv, kcode):
    groups = len(queries)
    keys = len(own_kv) * ROWS
    return pl.pallas_call(
        attend_own_kernel,
        in_specs=[pl.BlockSpec(memory_space=pltpu.VMEM)] * (2 + len(own_kv) + groups),
        out_shape=[
            jax.ShapeDtypeStruct((groups, HD, ROWS), jnp.float32),
            jax.ShapeDtypeStruct((groups, 8, ROWS), jnp.float32),
        ],
        scratch_shapes=[
            pltpu.VMEM((HD, keys), jnp.bfloat16),
            pltpu.VMEM((keys, 128), jnp.float32),
        ],
        compiler_params=pltpu.CompilerParams(vmem_limit_bytes=GRANT),
        name="attend_own",
    )(qcode, kcode, *own_kv, *queries)


def attend_other(queries, qcode, other_kv, kcode, own_mixed, own_stat):
    groups = len(queries)
    keys = other_kv.shape[0] * ROWS
    return pl.pallas_call(
        attend_other_kernel,
        in_specs=[pl.BlockSpec(memory_space=pltpu.VMEM)] * (5 + groups),
        out_shape=jax.ShapeDtypeStruct((groups, PART_ROWS, ROWS), jnp.bfloat16),
        scratch_shapes=[
            pltpu.VMEM((HD, keys), jnp.bfloat16),
            pltpu.VMEM((keys, 128), jnp.float32),
        ],
        compiler_params=pltpu.CompilerParams(vmem_limit_bytes=GRANT),
        name="attend_other",
    )(qcode, kcode, other_kv, own_mixed, own_stat, *queries)


def combine_kernel(part_ref, out_ref):
    groups = part_ref.shape[0]
    levels = []
    for j in range(groups):
        stats = part_ref[j, HD:].astype(jnp.float32)
        levels.append(stats[0:1] + stats[1:2] + stats[2:3])
    best = levels[0]
    for level in levels[1:]:
        best = jnp.maximum(best, level)
    total = jnp.zeros_like(best)
    mixed = jnp.zeros((HD, ROWS), jnp.float32)
    for j in range(groups):
        share = jnp.exp2(levels[j] - best)
        total = total + share
        mixed = mixed + share * part_ref[j, :HD].astype(jnp.float32)
    attended = jnp.transpose(mixed / total).astype(jnp.bfloat16)
    for j in range(out_ref.shape[0]):
        out_ref[j] = attended


def combine(parts, copies):
    return pl.pallas_call(
        combine_kernel,
        out_shape=jax.ShapeDtypeStruct((copies, ROWS, HD), jnp.bfloat16),
        compiler_params=pltpu.CompilerParams(vmem_limit_bytes=GRANT),
        name="combine",
    )(parts)


def split_kernel(w_ref, out_ref):
    parts, _, width = out_ref.shape
    for j in range(parts):
        out_ref[j] = w_ref[:, j * width : (j + 1) * width]


def split(w, parts):
    return pl.pallas_call(
        split_kernel,
        in_specs=[pl.BlockSpec(memory_space=pltpu.VMEM)],
        out_shape=jax.ShapeDtypeStruct((parts, HD, w.shape[1] // parts), w.dtype),
        compiler_params=pltpu.CompilerParams(vmem_limit_bytes=GRANT),
        name="split",
    )(w)


def output_kernel(attended_ref, w_ref, out_ref):
    total = jnp.zeros(out_ref.shape, jnp.float32)
    for h in range(attended_ref.shape[0]):
        head_out = jnp.dot(attended_ref[h], w_ref[h], preferred_element_type=jnp.float32)
        total = total + head_out.astype(jnp.bfloat16).astype(jnp.float32)
    out_ref[...] = total.astype(jnp.bfloat16)


def output(attended, w):
    return pl.pallas_call(
        output_kernel,
        in_specs=[pl.BlockSpec(memory_space=pltpu.VMEM)] * 2,
        out_shape=jax.ShapeDtypeStruct((ROWS, w.shape[2]), jnp.bfloat16),
        compiler_params=pltpu.CompilerParams(vmem_limit_bytes=GRANT),
        name="output",
    )(attended, w)


def make_on_device(n_seq, n_head):
    group = CORES * BLOCK_Z
    blocks = n_seq // group
    near = [
        [g * group + b * CORES + c for b in range(BLOCK_Z)] for g in range(blocks) for c in range(CORES)
    ]
    swap = [(i, i ^ 1) for i in range(n_seq)]
    keys = CORES * blocks * ROWS

    def codes(span_order, frame_id, camera_id):
        code = (frame_id * 8 + camera_id).reshape(-1, SPAN)[span_order]
        code = code.reshape(blocks, BLOCK_Z, CORES, ROWS)
        place = lax.axis_index("seq")
        core = place % CORES
        query_code = lax.dynamic_index_in_dim(code, place // group, 0, keepdims=False)
        query_code = lax.dynamic_index_in_dim(query_code, core, 1, keepdims=False)
        key_code = lax.dynamic_index_in_dim(code, place // CORES % BLOCK_Z, 1, keepdims=False)
        own = lax.dynamic_index_in_dim(key_code, core, 1, keepdims=False)
        other = lax.dynamic_index_in_dim(key_code, 1 - core, 1, keepdims=False)
        key_code = jnp.concatenate([own, other]).reshape(1, keys)
        row = lax.broadcasted_iota(jnp.int32, (16, keys), 0)
        pair = jnp.where(row == 0, key_code >> 3, jnp.where(row == 1, key_code & 7, 0))
        return query_code[:, None, :], pair.astype(jnp.bfloat16)

    along_block = [
        [(i, i // group * group + (i + k * CORES) % group) for i in range(n_seq)]
        for k in range(BLOCK_Z)
    ]
    across = [[(i, (i + k * group) % n_seq) for i in range(n_seq)] for k in range(blocks)]

    def on_device(tokens, norm_gain, w_qkv, w_out, span_order, frame_id, camera_id):
        copies = jnp.broadcast_to(tokens[None], (n_head,) + tokens.shape)
        gathered = lax.all_to_all(copies, "head", 0, 0)
        query_code, key_code = codes(span_order, frame_id, camera_id)
        w_split = split(w_out, n_head)
        w_heads = stage(w_qkv.transpose(1, 0, 2))
        gathered, w_split, w_heads, query_code, key_code = lax.optimization_barrier(
            (gathered, w_split, w_heads, query_code, key_code)
        )
        queries, kv = project(gathered, norm_gain.reshape(1, D), w_heads)
        own_kv = [kv] * blocks
        for k in (1, blocks - 1):
            own_kv[k] = lax.ppermute(kv, "seq", across[k])
        for k in range(2, blocks - 1):
            own_kv[k] = lax.ppermute(kv, "seq", across[k])
        all_queries = [queries]
        for k in range(1, BLOCK_Z):
            all_queries.append(lax.ppermute(queries, "seq", along_block[k]))
        w_columns = lax.all_to_all(w_split, "head", 0, 0)
        other_kv = lax.ppermute(jnp.stack(own_kv), "seq", swap)
        own_mixed, own_stat = attend_own(all_queries, query_code, own_kv, key_code)
        parts = attend_other(
            all_queries, query_code, other_kv, key_code, own_mixed, own_stat
        )
        parts, w_columns = lax.optimization_barrier((parts, w_columns))
        parts = lax.all_to_all(parts, "seq", 0, 0, axis_index_groups=near)
        attended = combine(parts, n_head)
        all_attended = lax.all_to_all(attended, "head", 0, 0)
        return output(all_attended, w_columns)

    return on_device


def solution(mesh):
    placed = (P("seq", "head"), P(), P(None, None, "head"), P("head", None), P(), P(), P())
    return jax.shard_map(
        make_on_device(mesh.shape["seq"], mesh.shape["head"]),
        mesh=mesh,
        in_specs=placed,
        out_specs=P("seq", "head"),
        check_vma=False,
    )
```
